256 devices in a mesh: lon: 32 (over y, x, core), lat: 8 (over z).
Axes of the slice: x: 4, y: 4, z: 8, core: 2. Of those that a mesh axis runs over, the one named last changes fastest.
Arguments:
- winds: bfloat16 [2, 32, 4, 1536, 1024], P(None, None, None, 'lon', 'lat'), may hold values from -60 to 60
Outputs:
- basis: float32 [48, 2, 4, 1536, 1024], P(None, None, None, 'lon', 'lat')
The draws below stay inside these ranges and needn't reach their ends.
All inputs are finite; a program needn't handle non-finite values.
Results may differ from the reference program's by a relative error of at most 0.0043.
Values may be sent and summed in bfloat16 or wider, within the bound.
No kernel may reach another device: no remote copies, remote signals or barrier semaphores. Data moves between devices by JAX's collectives and lax.ppermute only.
A program may use at most 128 MiB of HBM per device.

```python
import math
import jax
import jax.numpy as jnp
from jax import lax

LEV = 4
TIME = 32
TAPERS = 12
FREQS = 2
NLON = 1536
NLAT = 1024
ROWS = 12582912


def draw_winds(key, part):
    subkeys = jax.random.split(key, 3)
    shape = (2, TIME, LEV, NLON, NLAT)
    noise = jax.random.truncated_normal(subkeys[0], -4.0, 4.0, shape, jnp.float32)
    cell_scale = jnp.exp(jax.random.uniform(subkeys[1], (2, 1, LEV, NLON, NLAT), jnp.float32) * math.log(10.0))
    time_scale = jnp.exp(jax.random.uniform(subkeys[2], (2, TIME, 1, 1, 1), jnp.float32) * math.log(10.0))
    lon_ramp = 1.0 + 2.0 * jnp.arange(NLON, dtype=jnp.float32) / NLON
    return (noise * cell_scale * time_scale * lon_ramp[:, None] / 20.0).astype(jnp.bfloat16)


def setup_inputs(seed: int = 0) -> dict:
    key_of = jax.random.split(jax.random.key(seed), 2)
    winds = draw_winds(jax.random.fold_in(key_of[1], 71), 0)
    return dict(winds=winds)


def taper_table(times, tapers, freqs):
    times_f = jnp.arange(times, dtype=jnp.float32)
    order_k = jnp.arange(tapers, dtype=jnp.float32)
    weights = math.sqrt(2.0 / (times + 1)) * jnp.sin(math.pi * (order_k[:, None] + 1.0) * (times_f[None, :] + 1.0) / (times + 1))
    blocks = []
    for which in range(freqs):
        phases = 2.0 * math.pi * (7 + 2 * which) * times_f / times
        real_part = weights * jnp.cos(phases)[None, :]
        imag_part = -weights * jnp.sin(phases)[None, :]
        blocks.append(jnp.stack([real_part, imag_part], axis=1).reshape(2 * tapers, times))
    return jnp.concatenate(blocks, axis=0).astype(jnp.bfloat16)

def stencil(lon_pad, lat_pad, cos_lat, step_lon, step_lat):
    along_lon = (lon_pad[..., 2:, :].astype(jnp.float32) - lon_pad[..., :-2, :].astype(jnp.float32)) / (2.0 * step_lon)
    fluxes = lat_pad.astype(jnp.float32) * cos_lat
    along_lat = (fluxes[..., 2:] - fluxes[..., :-2]) / (2.0 * step_lat)
    middle = cos_lat[1:-1]
    vorticity = (along_lon[1] - along_lat[0]) / middle
    divergence = (along_lon[0] + along_lat[1]) / middle
    return jnp.stack([vorticity, divergence]).astype(jnp.bfloat16)

def reference(winds):
    step_lon = 2.0 * math.pi / NLON
    step_lat = 2.6 / NLAT
    lat_rows = jnp.arange(NLAT + 2, dtype=jnp.float32) - 1.0
    cos_lat = jnp.cos(-1.3 + (lat_rows + 0.5) * step_lat)
    table = taper_table(TIME, TAPERS, FREQS).astype(jnp.float32)

    def one_level(level_winds):
        lon_pad = jnp.concatenate([level_winds[..., -1:, :], level_winds, level_winds[..., :1, :]], axis=-2)
        zeros = jnp.zeros(level_winds.shape[:-1] + (1,), level_winds.dtype)
        lat_pad = jnp.concatenate([zeros, level_winds, zeros], axis=-1)
        fields = stencil(lon_pad, lat_pad, cos_lat, step_lon, step_lat)
        return jnp.einsum('ct,stxy->csxy', table, fields.astype(jnp.float32), precision=lax.Precision.HIGHEST)
    per_level = lax.map(one_level, jnp.moveaxis(winds, 2, 0))
    snapshots = jnp.moveaxis(per_level, 0, 2)
    columns = snapshots.reshape(FREQS, 2 * TAPERS, -1)
    gram = jnp.einsum('far,fbr->fab', columns, columns, precision=lax.Precision.HIGHEST) / ROWS
    factor = jnp.linalg.cholesky(gram)
    basis = jax.scipy.linalg.solve_triangular(factor, columns, lower=True)
    return basis.reshape(2 * FREQS * TAPERS, 2, LEV, NLON, NLAT)
```

```python
import functools
import math

import jax
import jax.numpy as jnp
import numpy as np
from jax import lax
from jax.experimental import pallas as pl
from jax.experimental.pallas import tpu as pltpu
from jax.sharding import Mesh
from jax.sharding import PartitionSpec as P

TIME = 32
TAPERS = 12
FREQS = 2
COLS = 2 * TAPERS
LON = ("lon_0", "lon_1", "lon_2")
SUB = 8
F32 = jnp.float32
BF16 = jnp.bfloat16


def taper_table():
    t = np.arange(TIME, dtype=np.float32)
    k = np.arange(TAPERS, dtype=np.float32)
    weights = np.float32(math.sqrt(2.0 / (TIME + 1))) * np.sin(
        np.float32(math.pi)
        * (k[:, None] + np.float32(1.0))
        * (t[None, :] + np.float32(1.0))
        / np.float32(TIME + 1)
    )
    blocks = []
    for which in range(FREQS):
        phases = np.float32(2.0 * math.pi * (7 + 2 * which)) * t / np.float32(TIME)
        real_part = weights * np.cos(phases)[None, :]
        imag_part = -weights * np.sin(phases)[None, :]
        blocks.append(np.stack([real_part, imag_part], axis=1).reshape(COLS, TIME))
    return np.concatenate(blocks, axis=0).astype(jnp.bfloat16).astype(np.float32)


def iota(shape, dim):
    return lax.broadcasted_iota(jnp.int32, shape, dim)


def pack_kernel(w_ref, first_ref, last_ref, cols_ref, acc_ref):
    level = pl.program_id(0)
    comps, times, _, rows, lanes = w_ref.shape
    groups = rows // SUB
    deep = times * SUB
    pieces = []
    for c in range(comps):
        for g in range(groups):
            x = w_ref[c, :, 0, g * SUB : (g + 1) * SUB, :].astype(F32)
            pieces.append(x.reshape(deep, lanes).astype(BF16))
    t_of = iota((times, deep), 0) * SUB
    at = iota((times, deep), 1)
    pick_first = (at == t_of).astype(F32).astype(BF16)
    pick_last = (at == t_of + SUB - 1).astype(F32).astype(BF16)
    for c in range(comps):
        lo = jnp.dot(pick_first, pieces[c * groups], preferred_element_type=F32)
        hi = jnp.dot(pick_last, pieces[c * groups + groups - 1], preferred_element_type=F32)
        first_ref[c * times : (c + 1) * times, :] = lo.astype(BF16)
        last_ref[c * times : (c + 1) * times, :] = hi.astype(BF16)

    src = iota((lanes, lanes), 0)
    dst = iota((lanes, lanes), 1)
    blocks = comps * groups
    total = jnp.zeros((deep, lanes), F32)
    for b in range(blocks):
        spot = 2 * (level * blocks + b)
        hit = ((src == lanes - 1) & (dst == spot)) | ((src == 0) & (dst == spot + 1))
        total += jnp.dot(pieces[b], hit.astype(F32).astype(BF16), preferred_element_type=F32)

    @pl.when(level == 0)
    def _():
        acc_ref[...] = total

    @pl.when(level > 0)
    def _():
        acc_ref[...] += total

    @pl.when(level == pl.num_programs(0) - 1)
    def _():
        cols_ref[...] = acc_ref[...].astype(BF16)


def pack(winds):
    comps, times, levels, rows, lanes = winds.shape
    edge = jax.ShapeDtypeStruct((levels * comps * times, lanes), BF16)
    edge_spec = pl.BlockSpec((comps * times, lanes), lambda l: (l, 0))
    return pl.pallas_call(
        pack_kernel,
        grid=(levels,),
        in_specs=[pl.BlockSpec((comps, times, 1, rows, lanes), lambda l: (0, 0, l, 0, 0))],
        out_specs=[edge_spec, edge_spec, pl.BlockSpec((times * SUB, lanes), lambda l: (0, 0))],
        out_shape=[edge, edge, jax.ShapeDtypeStruct((times * SUB, lanes), BF16)],
        scratch_shapes=[pltpu.VMEM((times * SUB, lanes), F32)],
        compiler_params=pltpu.CompilerParams(vmem_limit_bytes=24 << 20),
        name="pack",
    )(winds)


def fields_kernel(
    step_lon, step_lat, w_ref, prev_ref, next_ref, left_ref, right_ref, cos_ref,
    f_ref, c_ref, prev_s, next_s, side_s, acc_ref,
):
    level = pl.program_id(0)
    comps, times, _, rows, lanes = w_ref.shape
    groups = rows // SUB
    deep = times * SUB
    blocks = comps * groups

    prev_s[...] = prev_ref[...].astype(F32)
    next_s[...] = next_ref[...].astype(F32)
    odd = iota((deep, lanes), 1) % 2 == 1
    side_s[...] = jnp.where(odd, right_ref[...].astype(F32), left_ref[...].astype(F32))

    cos_row = cos_ref[1:2, :]
    by_lon = jnp.broadcast_to(1.0 / (2.0 * step_lon) / cos_row, (rows, lanes))
    by_up = jnp.broadcast_to(cos_ref[2:3, :] / (2.0 * step_lat) / cos_row, (rows, lanes))
    by_down = jnp.broadcast_to(cos_ref[0:1, :] / (2.0 * step_lat) / cos_row, (rows, lanes))
    row = iota((rows, lanes), 0)
    lane = iota((rows, lanes), 1)

    def shifted(c, t):
        x = w_ref[c, t, 0].astype(F32)
        below = jnp.where(row == 0, prev_s[pl.ds(c * times + t, 1), :], pltpu.roll(x, 1, 0))
        above = jnp.where(row == rows - 1, next_s[pl.ds(c * times + t, 1), :], pltpu.roll(x, rows - 1, 0))
        halo = side_s[pl.ds(pl.multiple_of(t * SUB, SUB), SUB), :]
        parts = []
        for g in range(groups):
            spot = 2 * (level * blocks + c * groups + g) + 1
            parts.append(pltpu.roll(halo, lanes - spot, 1))
        halo = jnp.concatenate(parts, axis=0)
        west = pltpu.roll(jnp.where(lane == lanes - 1, halo, x), 1, 1)
        east = pltpu.roll(jnp.where(lane == 0, halo, x), lanes - 1, 1)
        return (above - below) * by_lon, east * by_up - west * by_down

    def one(t):
        u_lon, u_lat = shifted(0, t)
        v_lon, v_lat = shifted(1, t)
        return v_lon - u_lat, u_lon + v_lat

    @pl.loop(0, times // 2)
    def _(pair):
        even = one(2 * pair)
        later = one(2 * pair + 1)
        at = pl.ds(pl.multiple_of(pair * 2 * SUB, 2 * SUB), 2 * SUB)
        for s in range(2):
            for g in range(groups):
                cut = slice(g * SUB, (g + 1) * SUB)
                both = jnp.concatenate([even[s][cut], later[s][cut]], axis=0)
                f_ref[0, s, g, at, :] = both.astype(BF16)

    total = None
    for s in range(2):
        x = jnp.concatenate([f_ref[0, s, g] for g in range(groups)], axis=1)
        term = lax.dot_general(x, x, (((1,), (1,)), ((), ())), preferred_element_type=F32)
        total = term if total is None else total + term

    @pl.when(level == 0)
    def _():
        acc_ref[...] = total

    @pl.when(level > 0)
    def _():
        acc_ref[...] += total

    @pl.when(level == pl.num_programs(0) - 1)
    def _():
        same = iota((deep, deep), 0) % SUB == iota((deep, deep), 1) % SUB
        kept = jnp.where(same, acc_ref[...], 0.0)
        kept = kept.reshape(times, SUB, deep).sum(axis=1)
        fold = (iota((deep, times), 0) // SUB == iota((deep, times), 1)).astype(F32)
        cov = jnp.dot(kept, fold, precision=lax.Precision.HIGHEST, preferred_element_type=F32)
        c_ref[...] = jnp.concatenate([cov[q * SUB : (q + 1) * SUB] for q in range(times // SUB)], axis=1)


def fields(winds, prev_row, next_row, left, right, cos_rows, step_lon, step_lat):
    comps, times, levels, rows, lanes = winds.shape
    groups = rows // SUB
    deep = times * SUB
    edge_spec = pl.BlockSpec((comps * times, lanes), lambda l: (l, 0))
    side_spec = pl.BlockSpec((deep, lanes), lambda l: (0, 0))
    return pl.pallas_call(
        functools.partial(fields_kernel, step_lon, step_lat),
        grid=(levels,),
        in_specs=[
            pl.BlockSpec((comps, times, 1, rows, lanes), lambda l: (0, 0, l, 0, 0)),
            edge_spec, edge_spec, side_spec, side_spec,
            pl.BlockSpec((SUB, lanes), lambda l: (0, 0)),
        ],
        out_specs=[
            pl.BlockSpec((1, 2, groups, deep, lanes), lambda l: (l, 0, 0, 0, 0)),
            pl.BlockSpec((SUB, lanes), lambda l: (0, 0)),
        ],
        out_shape=[
            jax.ShapeDtypeStruct((levels, 2, groups, deep, lanes), BF16),
            jax.ShapeDtypeStruct((SUB, lanes), F32),
        ],
        scratch_shapes=[
            pltpu.VMEM((comps * times, lanes), F32),
            pltpu.VMEM((comps * times, lanes), F32),
            pltpu.VMEM((deep, lanes), F32),
            pltpu.VMEM((deep, deep), F32),
        ],
        compiler_params=pltpu.CompilerParams(vmem_limit_bytes=24 << 20),
        name="fields",
    )(winds, prev_row, next_row, left, right, cos_rows)


def basis_kernel(total_rows, sums_ref, table_ref, f_ref, out_ref, hi_ref, lo_ref):
    _, _, groups, deep, lanes = f_ref.shape
    times = deep // SUB
    outs = FREQS * COLS

    @pl.when((pl.program_id(0) == 0) & (pl.program_id(1) == 0))
    def _():
        half = lanes // 2
        flat = jnp.sum(sums_ref[...], axis=0)
        cov = jnp.concatenate([flat[:, q * times : (q + 1) * times] for q in range(times // SUB)], axis=0)
        table = table_ref[...]
        high = lax.Precision.HIGHEST
        left = jnp.dot(table, cov, precision=high, preferred_element_type=F32)
        gram = lax.dot_general(
            left, table, (((1,), (1,)), ((), ())), precision=high, preferred_element_type=F32
        ) / total_rows
        pad = jnp.zeros((COLS, half - COLS - times), F32)
        parts = []
        for f in range(FREQS):
            at = slice(f * COLS, (f + 1) * COLS)
            parts += [gram[at, at], table[at], pad]
        a = jnp.concatenate(parts, axis=1)
        row = iota((COLS, lanes), 0)
        lane = iota((COLS, lanes), 1)
        near = lane < half
        for j in range(COLS):
            pivot_row = a[j : j + 1, :]
            inv0 = 1.0 / pivot_row[:, j : j + 1]
            inv1 = 1.0 / pivot_row[:, half + j : half + j + 1]
            m = jnp.where(near, a[:, j : j + 1] * inv0, a[:, half + j : half + j + 1] * inv1)
            a = a - jnp.where(row > j, m, 0.0) * pivot_row
        rows = []
        for f in range(FREQS):
            d = jnp.sum(jnp.where(lane == f * half + row, a, 0.0), axis=1, keepdims=True)
            rows.append(a[:, f * half + COLS : f * half + COLS + times] / jnp.sqrt(d))
        w = jnp.concatenate(rows, axis=0)
        w_hi = w.astype(BF16)
        w_lo = (w - w_hi.astype(F32)).astype(BF16)
        spread = (iota((outs * SUB, outs), 0) // SUB == iota((outs * SUB, outs), 1)).astype(F32).astype(BF16)
        widen = (iota((times, deep), 0) == iota((times, deep), 1) // SUB).astype(F32).astype(BF16)
        same = iota((outs * SUB, deep), 0) % SUB == iota((outs * SUB, deep), 1) % SUB
        for term, ref in ((w_hi, hi_ref), (w_lo, lo_ref)):
            tall = jnp.dot(spread, term, preferred_element_type=F32).astype(BF16)
            full = jnp.dot(tall, widen, preferred_element_type=F32)
            ref[...] = jnp.where(same, full, 0.0).astype(BF16)

    for g in range(0, groups, 2):
        x = jnp.concatenate([f_ref[0, 0, g], f_ref[0, 0, g + 1]], axis=1)
        y = jnp.dot(hi_ref[...], x, preferred_element_type=F32)
        y += jnp.dot(lo_ref[...], x, preferred_element_type=F32)
        for e in range(2):
            part = y[:, e * lanes : (e + 1) * lanes].reshape(outs, SUB, lanes)
            out_ref[:, 0, 0, (g + e) * SUB : (g + e + 1) * SUB, :] = part


def basis_of(sums, table, f, total_rows):
    levels, kinds, groups, deep, lanes = f.shape
    outs = FREQS * COLS
    return pl.pallas_call(
        functools.partial(basis_kernel, total_rows),
        grid=(kinds, levels),
        in_specs=[
            pl.BlockSpec(sums.shape, lambda s, l: (0, 0, 0)),
            pl.BlockSpec(table.shape, lambda s, l: (0, 0)),
            pl.BlockSpec((1, 1, groups, deep, lanes), lambda s, l: (l, s, 0, 0, 0)),
        ],
        out_specs=pl.BlockSpec((outs, 1, 1, groups * SUB, lanes), lambda s, l: (0, s, l, 0, 0)),
        out_shape=jax.ShapeDtypeStruct((outs, kinds, levels, groups * SUB, lanes), F32),
        scratch_shapes=[
            pltpu.VMEM((outs * SUB, deep), BF16),
            pltpu.VMEM((outs * SUB, deep), BF16),
        ],
        compiler_params=pltpu.CompilerParams(vmem_limit_bytes=24 << 20),
        name="basis",
    )(sums, table, f)


def exchange(x, axes):
    copies = jnp.broadcast_to(x, (lax.axis_size(axes), *x.shape))
    return lax.all_to_all(copies, axes, split_axis=0, concat_axis=0, tiled=True)


def ring(x, axes, step):
    size = lax.axis_size(axes)
    return lax.ppermute(x, axes, [(i, (i + step) % size) for i in range(size)])


def body(winds):
    _, times, levels, lon_cells, lat_cells = winds.shape
    grid_lon = lon_cells * lax.axis_size(LON)
    grid_lat = lat_cells * lax.axis_size("lat")
    step_lon = 2.0 * math.pi / grid_lon
    step_lat = 2.6 / grid_lat
    first, last, cols = pack(winds)
    prev_row = ring(last, LON, 1)
    next_row = ring(first, LON, -1)
    left = ring(cols, "lat", 1)
    right = ring(cols, "lat", -1)
    shape = (SUB, lat_cells)
    index = lax.axis_index("lat") * lat_cells + iota(shape, 1) + iota(shape, 0) - 1
    inside = (index >= 0) & (index < grid_lat)
    cos_rows = jnp.where(inside, jnp.cos(-1.3 + (index.astype(F32) + 0.5) * step_lat), 0.0)
    f, cov = fields(winds, prev_row, next_row, left, right, cos_rows, step_lon, step_lat)
    near = exchange(cov, ("lon_2", "lat")).sum(axis=0)
    sums = exchange(near, ("lon_0", "lon_1"))
    return basis_of(sums, jnp.asarray(taper_table()), f, 2 * levels * grid_lon * grid_lat)


def solution(mesh):
    split = Mesh(
        mesh.devices.reshape(4, 4, 2, mesh.shape["lat"]), ("lon_0", "lon_1", "lon_2", "lat")
    )
    placed = (P(None, None, None, LON, "lat"),)
    return jax.shard_map(
        body,
        mesh=split,
        in_specs=placed,
        out_specs=P(None, None, None, LON, "lat"),
        check_vma=False,
    )
```

```python
import functools
import math

import jax
import jax.numpy as jnp
import numpy as np
from jax import lax
from jax.experimental import pallas as pl
from jax.experimental.pallas import tpu as pltpu
from jax.sharding import Mesh
from jax.sharding import PartitionSpec as P

TIME = 32
TAPERS = 12
FREQS = 2
COLS = 2 * TAPERS
LON = ("lon_0", "lon_1", "lon_2")
SUB = 8
BIG = 16
F32 = jnp.float32
BF16 = jnp.bfloat16


def taper_table():
    t = np.arange(TIME, dtype=np.float32)
    k = np.arange(TAPERS, dtype=np.float32)
    weights = np.float32(math.sqrt(2.0 / (TIME + 1))) * np.sin(
        np.float32(math.pi)
        * (k[:, None] + np.float32(1.0))
        * (t[None, :] + np.float32(1.0))
        / np.float32(TIME + 1)
    )
    blocks = []
    for which in range(FREQS):
        phases = np.float32(2.0 * math.pi * (7 + 2 * which)) * t / np.float32(TIME)
        real_part = weights * np.cos(phases)[None, :]
        imag_part = -weights * np.sin(phases)[None, :]
        blocks.append(np.stack([real_part, imag_part], axis=1).reshape(COLS, TIME))
    return np.concatenate(blocks, axis=0).astype(jnp.bfloat16).astype(np.float32)


def iota(shape, dim):
    return lax.broadcasted_iota(jnp.int32, shape, dim)


def unit_columns(comps, thirds, halves):
    return comps * thirds * halves


def shift_table(lanes, units):
    table = np.zeros((units, 2 * lanes, 2 * lanes), np.float32)
    j = np.arange(lanes - 1)
    table[:, j + 1, j] = 1.0
    table[:, j, lanes + j + 1] = 1.0
    for u in range(units):
        table[u, lanes + 2 * u + 1, lanes - 1] = 1.0
        table[u, lanes + 2 * u, lanes] = 1.0
    return table.astype(jnp.bfloat16)


def pack_kernel(w_hbm, first_ref, last_ref, cols_ref, w_ref, first_s, last_s, acc_ref, sems):
    comps, times, levels, rows, lanes = w_ref.shape
    half = times // 2
    thirds = rows // BIG
    units = unit_columns(comps, thirds, 2)
    copies = [
        pltpu.make_async_copy(w_hbm.at[:, :, l], w_ref.at[:, :, l], sems.at[l]) for l in range(levels)
    ]
    for copy in copies:
        copy.start()
    deep = half * BIG
    at = iota((units * lanes, lanes), 0)
    spot = iota((units * lanes, lanes), 1)
    here = at % lanes
    want = at // lanes * 2
    hit = ((here == lanes - 1) & (spot == want)) | ((here == 0) & (spot == want + 1))
    hit = hit.astype(F32).astype(BF16)
    for l in range(levels):
        copies[l].wait()
        pieces = []
        for c in range(comps):
            for g in range(thirds):
                for h in range(2):
                    x = w_ref[c, h * half : (h + 1) * half, l, g * BIG : (g + 1) * BIG, :]
                    pieces.append(x.reshape(deep, lanes))
            for t in range(times):
                k = (l * comps + c) * times + t
                first_s[k : k + 1, :] = w_ref[c, t, l, 0:BIG, :].astype(F32)[0:1]
                last_s[k : k + 1, :] = w_ref[c, t, l, rows - BIG : rows, :].astype(F32)[BIG - 1 : BIG]
        total = jnp.dot(jnp.concatenate(pieces, axis=1), hit, preferred_element_type=F32)
        if l == 0:
            acc_ref[...] = total
        else:
            acc_ref[...] += pltpu.roll(total, 2 * units * l, 1)
    cols_ref[...] = acc_ref[...].astype(BF16)
    first_ref[...] = first_s[...].astype(BF16)
    last_ref[...] = last_s[...].astype(BF16)


def pack(winds):
    comps, times, levels, rows, lanes = winds.shape
    deep = times // 2 * BIG
    many = levels * comps * times
    edge = jax.ShapeDtypeStruct((many, lanes), BF16)
    return pl.pallas_call(
        pack_kernel,
        in_specs=[pl.BlockSpec(memory_space=pltpu.HBM)],
        out_shape=[edge, edge, jax.ShapeDtypeStruct((deep, lanes), BF16)],
        scratch_shapes=[
            pltpu.VMEM(winds.shape, BF16),
            pltpu.VMEM((many, lanes), F32),
            pltpu.VMEM((many, lanes), F32),
            pltpu.VMEM((deep, lanes), F32),
            pltpu.SemaphoreType.DMA((levels,)),
        ],
        compiler_params=pltpu.CompilerParams(vmem_limit_bytes=24 << 20),
        name="pack",
    )(pltpu.with_memory_space_constraint(winds, pltpu.HBM))


def fields_kernel(
    step_lon, step_lat, w_ref, prev_ref, next_ref, left_ref, right_ref, cos_ref, shift_ref,
    f_hbm, c_ref, prev_s, next_s, side_s, moved_s, f_ref, acc_ref, sems,
):
    comps, times, levels, rows, lanes = w_ref.shape
    groups = rows // SUB
    thirds = rows // BIG
    half = times // 2
    deep = times * SUB
    units = unit_columns(comps, thirds, 2)

    prev_s[...] = prev_ref[...].astype(F32)
    next_s[...] = next_ref[...].astype(F32)
    odd = iota(left_ref.shape, 1) % 2 == 1
    side = jnp.where(odd, right_ref[...].astype(F32), left_ref[...].astype(F32))
    for l in range(levels):
        mine = side if l == 0 else pltpu.roll(side, lanes - 2 * units * l, 1)
        side_s[l] = mine.astype(BF16)

    cos_row = cos_ref[1:2, :]
    by_lon = jnp.broadcast_to(1.0 / (2.0 * step_lon) / cos_row, (SUB, lanes))
    by_up = jnp.broadcast_to(cos_ref[2:3, :] / (2.0 * step_lat) / cos_row, (SUB, lanes))
    by_down = jnp.broadcast_to(cos_ref[0:1, :] / (2.0 * step_lat) / cos_row, (SUB, lanes))
    row = iota((SUB, lanes), 0)
    copies = [pltpu.make_async_copy(f_ref.at[l], f_hbm.at[l], sems.at[l]) for l in range(levels)]

    @pl.loop(0, levels)
    def _(l):
        edge = side_s[l]
        for h in range(2):
            for c in range(comps):
                for g in range(thirds):
                    x = w_ref[c, h * half : (h + 1) * half, l, g * BIG : (g + 1) * BIG, :]
                    x = jnp.concatenate([x.reshape(half * BIG, lanes), edge], axis=1)
                    moved_s[h, c, g] = jnp.dot(
                        x, shift_ref[(c * thirds + g) * 2 + h], preferred_element_type=F32
                    )

        def one(t):
            h = t // half
            by = {}
            for c in range(comps):
                x = w_ref[c, t, l].astype(F32)
                k = (l * comps + c) * times + t
                tiles = [x[g * SUB : (g + 1) * SUB] for g in range(groups)]
                up = [pltpu.roll(v, SUB - 1, 0) for v in tiles]
                down = [pltpu.roll(v, 1, 0) for v in tiles]
                up.append(jnp.broadcast_to(next_s[pl.ds(k, 1), :], (SUB, lanes)))
                down.append(jnp.broadcast_to(prev_s[pl.ds(k, 1), :], (SUB, lanes)))
                for g in range(groups):
                    above = jnp.where(row == SUB - 1, up[g + 1], up[g])
                    below = jnp.where(row == 0, down[g - 1], down[g])
                    at = (t % half) * BIG + g % 2 * SUB
                    east = moved_s[h, c, g // 2, at : at + SUB, :lanes]
                    west = moved_s[h, c, g // 2, at : at + SUB, lanes:]
                    by[c, g] = ((above - below) * by_lon, east * by_up - west * by_down)
            return [
                [by[1, g][0] - by[0, g][1] for g in range(groups)],
                [by[0, g][0] + by[1, g][1] for g in range(groups)],
            ]

        for pair in range(times // 2):
            even, later = one(2 * pair), one(2 * pair + 1)
            at = pair * 2 * SUB
            for s in range(2):
                for g in range(groups):
                    both = jnp.concatenate([even[s][g], later[s][g]], axis=0)
                    f_ref[l, s, g, at : at + 2 * SUB, :] = both.astype(BF16)

        total = None
        for s in range(2):
            x = jnp.concatenate([f_ref[l, s, g] for g in range(groups)], axis=1)
            term = lax.dot_general(x, x, (((1,), (1,)), ((), ())), preferred_element_type=F32)
            total = term if total is None else total + term

        @pl.when(l == 0)
        def _():
            acc_ref[...] = total

        @pl.when(l > 0)
        def _():
            acc_ref[...] += total

        pltpu.make_async_copy(f_ref.at[l], f_hbm.at[l], sems.at[l]).start()

    same = iota((deep, deep), 0) % SUB == iota((deep, deep), 1) % SUB
    kept = jnp.where(same, acc_ref[...], 0.0)
    kept = kept.reshape(times, SUB, deep).sum(axis=1)
    fold = (iota((deep, times), 0) // SUB == iota((deep, times), 1)).astype(F32)
    cov = jnp.dot(kept, fold, precision=lax.Precision.HIGHEST, preferred_element_type=F32)
    c_ref[...] = jnp.concatenate([cov[q * SUB : (q + 1) * SUB] for q in range(times // SUB)], axis=1)
    for copy in copies:
        copy.wait()


def fields(winds, prev_row, next_row, left, right, cos_rows, step_lon, step_lat):
    comps, times, levels, rows, lanes = winds.shape
    groups = rows // SUB
    thirds = rows // BIG
    deep = times * SUB
    shifts = jnp.asarray(shift_table(lanes, unit_columns(comps, thirds, 2)))
    whole = pl.BlockSpec(memory_space=pltpu.VMEM)
    f_shape = (levels, 2, groups, deep, lanes)
    return pl.pallas_call(
        functools.partial(fields_kernel, step_lon, step_lat),
        in_specs=[whole] * 7,
        out_specs=[pl.BlockSpec(memory_space=pltpu.HBM), whole],
        out_shape=[pltpu.HBM(f_shape, BF16), jax.ShapeDtypeStruct((SUB, lanes), F32)],
        scratch_shapes=[
            pltpu.VMEM(prev_row.shape, F32),
            pltpu.VMEM(prev_row.shape, F32),
            pltpu.VMEM((levels, *left.shape), BF16),
            pltpu.VMEM((2, comps, thirds, times // 2 * BIG, 2 * lanes), F32),
            pltpu.VMEM(f_shape, BF16),
            pltpu.VMEM((deep, deep), F32),
            pltpu.SemaphoreType.DMA((levels,)),
        ],
        compiler_params=pltpu.CompilerParams(vmem_limit_bytes=32 << 20),
        name="fields",
    )(winds, prev_row, next_row, left, right, cos_rows, shifts)


def basis_kernel(total_rows, sums_ref, table_ref, f_hbm, out_hbm, f_ref, out_ref, mix_ref, in_sems, out_sems):
    levels, kinds, groups, deep, lanes = f_ref.shape
    times = deep // SUB
    outs = FREQS * COLS
    for k in range(levels):
        pltpu.make_async_copy(f_hbm.at[k], f_ref.at[k], in_sems.at[k]).start()

    half = lanes // 2
    flat = jnp.sum(sums_ref[...], axis=0)
    cov = jnp.concatenate([flat[:, q * times : (q + 1) * times] for q in range(times // SUB)], axis=0)
    table = table_ref[...]
    high = lax.Precision.HIGHEST
    left = jnp.dot(table, cov, precision=high, preferred_element_type=F32)
    gram = lax.dot_general(
        left, table, (((1,), (1,)), ((), ())), precision=high, preferred_element_type=F32
    ) / total_rows
    pad = jnp.zeros((COLS, half - COLS - times), F32)
    parts = []
    for f in range(FREQS):
        at = slice(f * COLS, (f + 1) * COLS)
        parts += [gram[at, at], table[at], pad]
    a = jnp.concatenate(parts, axis=1)
    row = iota((COLS, lanes), 0)
    lane = iota((COLS, lanes), 1)
    near = lane < half
    for j in range(COLS):
        pivot_row = a[j : j + 1, :]
        inv0 = 1.0 / pivot_row[:, j : j + 1]
        inv1 = 1.0 / pivot_row[:, half + j : half + j + 1]
        m = jnp.where(near, a[:, j : j + 1] * inv0, a[:, half + j : half + j + 1] * inv1)
        a = a - jnp.where(row > j, m, 0.0) * pivot_row
    rows = []
    for f in range(FREQS):
        d = jnp.sum(jnp.where(lane == f * half + row, a, 0.0), axis=1, keepdims=True)
        rows.append(a[:, f * half + COLS : f * half + COLS + times] / jnp.sqrt(d))
    w = jnp.concatenate(rows, axis=0)
    w_hi = w.astype(BF16)
    w_lo = (w - w_hi.astype(F32)).astype(BF16)
    spread = (iota((outs * SUB, outs), 0) // SUB == iota((outs * SUB, outs), 1)).astype(F32).astype(BF16)
    widen = (iota((times, deep), 0) == iota((times, deep), 1) // SUB).astype(F32).astype(BF16)
    same = iota((outs * SUB, deep), 0) % SUB == iota((outs * SUB, deep), 1) % SUB
    for k, term in enumerate((w_hi, w_lo)):
        tall = jnp.dot(spread, term, preferred_element_type=F32).astype(BF16)
        full = jnp.dot(tall, widen, preferred_element_type=F32)
        mix_ref[:, k * deep : (k + 1) * deep] = jnp.where(same, full, 0.0).astype(BF16)

    @pl.loop(0, levels)
    def _(l):
        pltpu.make_async_copy(f_hbm.at[l], f_ref.at[l], in_sems.at[l]).wait()
        for s in range(kinds):
            for g in range(0, groups, 2):
                x = jnp.concatenate([f_ref[l, s, g], f_ref[l, s, g + 1]], axis=1)
                x = jnp.concatenate([x, x], axis=0)
                y = jnp.dot(mix_ref[...], x, preferred_element_type=F32)
                for e in range(2):
                    part = y[:, e * lanes : (e + 1) * lanes].reshape(outs, SUB, lanes)
                    out_ref[:, s, l, (g + e) * SUB : (g + e + 1) * SUB, :] = part
            pltpu.make_async_copy(out_ref.at[:, s, l], out_hbm.at[:, s, l], out_sems.at[s, l]).start()

    for l in range(levels):
        for s in range(kinds):
            pltpu.make_async_copy(out_ref.at[:, s, l], out_hbm.at[:, s, l], out_sems.at[s, l]).wait()


def basis_of(sums, table, f, total_rows):
    levels, kinds, groups, deep, lanes = f.shape
    outs = FREQS * COLS
    whole = pl.BlockSpec(memory_space=pltpu.VMEM)
    out_shape = (outs, kinds, levels, groups * SUB, lanes)
    return pl.pallas_call(
        functools.partial(basis_kernel, total_rows),
        in_specs=[whole, whole, pl.BlockSpec(memory_space=pltpu.HBM)],
        out_specs=pl.BlockSpec(memory_space=pltpu.HBM),
        out_shape=pltpu.HBM(out_shape, F32),
        scratch_shapes=[
            pltpu.VMEM(f.shape, BF16),
            pltpu.VMEM(out_shape, F32),
            pltpu.VMEM((outs * SUB, 2 * deep), BF16),
            pltpu.SemaphoreType.DMA((levels,)),
            pltpu.SemaphoreType.DMA((kinds, levels)),
        ],
        compiler_params=pltpu.CompilerParams(vmem_limit_bytes=32 << 20),
        name="basis",
    )(sums, table, f)


def exchange(x, axes):
    copies = jnp.broadcast_to(x, (lax.axis_size(axes), *x.shape))
    return lax.all_to_all(copies, axes, split_axis=0, concat_axis=0, tiled=True)


def ring(x, axes, step):
    size = lax.axis_size(axes)
    return lax.ppermute(x, axes, [(i, (i + step) % size) for i in range(size)])


def body(winds):
    _, times, levels, lon_cells, lat_cells = winds.shape
    grid_lon = lon_cells * lax.axis_size(LON)
    grid_lat = lat_cells * lax.axis_size("lat")
    step_lon = 2.0 * math.pi / grid_lon
    step_lat = 2.6 / grid_lat
    first, last, cols = pack(winds)
    prev_row = ring(last, LON, 1)
    next_row = ring(first, LON, -1)
    left = ring(cols, "lat", 1)
    right = ring(cols, "lat", -1)
    shape = (SUB, lat_cells)
    index = lax.axis_index("lat") * lat_cells + iota(shape, 1) + iota(shape, 0) - 1
    inside = (index >= 0) & (index < grid_lat)
    cos_rows = jnp.where(inside, jnp.cos(-1.3 + (index.astype(F32) + 0.5) * step_lat), 0.0)
    f, cov = fields(winds, prev_row, next_row, left, right, cos_rows, step_lon, step_lat)
    near = exchange(cov, ("lon_2", "lat")).sum(axis=0)
    sums = exchange(near, ("lon_0", "lon_1"))
    return basis_of(sums, jnp.asarray(taper_table()), f, 2 * levels * grid_lon * grid_lat)


def solution(mesh):
    split = Mesh(
        mesh.devices.reshape(4, 4, 2, mesh.shape["lat"]), ("lon_0", "lon_1", "lon_2", "lat")
    )
    placed = (P(None, None, None, LON, "lat"),)
    return jax.shard_map(
        body,
        mesh=split,
        in_specs=placed,
        out_specs=P(None, None, None, LON, "lat"),
        check_vma=False,
    )
```

```python
import functools
import math

import jax
import jax.numpy as jnp
import numpy as np
from jax import lax
from jax.experimental import pallas as pl
from jax.experimental.pallas import tpu as pltpu
from jax.sharding import Mesh
from jax.sharding import PartitionSpec as P

TIME = 32
TAPERS = 12
FREQS = 2
COLS = 2 * TAPERS
LON = ("lon_0", "lon_1", "lon_2")
SUB = 8
BIG = 16
F32 = jnp.float32
BF16 = jnp.bfloat16


def taper_table():
    t = np.arange(TIME, dtype=np.float32)
    k = np.arange(TAPERS, dtype=np.float32)
    weights = np.float32(math.sqrt(2.0 / (TIME + 1))) * np.sin(
        np.float32(math.pi)
        * (k[:, None] + np.float32(1.0))
        * (t[None, :] + np.float32(1.0))
        / np.float32(TIME + 1)
    )
    blocks = []
    for which in range(FREQS):
        phases = np.float32(2.0 * math.pi * (7 + 2 * which)) * t / np.float32(TIME)
        real_part = weights * np.cos(phases)[None, :]
        imag_part = -weights * np.sin(phases)[None, :]
        blocks.append(np.stack([real_part, imag_part], axis=1).reshape(COLS, TIME))
    return np.concatenate(blocks, axis=0).astype(jnp.bfloat16).astype(np.float32)


def iota(shape, dim):
    return lax.broadcasted_iota(jnp.int32, shape, dim)


def parity(axis):
    return lax.axis_index(axis) % 2


def as_bf16(mask):
    return mask.astype(F32).astype(BF16)


def three_terms(x):
    first = x.astype(BF16)
    rest = x - first.astype(F32)
    second = rest.astype(BF16)
    third = (rest - second.astype(F32)).astype(BF16)
    return first, second, third


def unit_of(c, g, h, thirds):
    return (c * thirds + g) * 2 + h


def pack_kernel(
    w_hbm, near_ref, far_ref, cols_ref, w_ref, first_s, last_s, acc_ref, sems,
):
    comps, times, levels, rows, lanes = w_ref.shape
    half = times // 2
    thirds = rows // BIG
    units = comps * thirds * 2
    copies = [
        pltpu.make_async_copy(w_hbm.at[:, :, l], w_ref.at[:, :, l], sems.at[l]) for l in range(levels)
    ]
    for copy in copies:
        copy.start()
    deep = half * BIG
    at = iota((units * lanes, lanes), 0)
    spot = iota((units * lanes, lanes), 1)
    here = at % lanes
    want = at // lanes * 2
    hit = as_bf16(((here == lanes - 1) & (spot == want)) | ((here == 0) & (spot == want + 1)))
    for l in range(levels):
        copies[l].wait()
        pieces = []
        for c in range(comps):
            for g in range(thirds):
                for h in range(2):
                    x = w_ref[c, h * half : (h + 1) * half, l, g * BIG : (g + 1) * BIG, :]
                    pieces.append(x.reshape(deep, lanes))
            for t in range(times):
                k = (l * comps + c) * times + t
                first_s[k : k + 1, :] = w_ref[c, t, l, 0:BIG, :].astype(F32)[0:1]
                last_s[k : k + 1, :] = w_ref[c, t, l, rows - BIG : rows, :].astype(F32)[BIG - 1 : BIG]
        total = jnp.dot(jnp.concatenate(pieces, axis=1), hit, preferred_element_type=F32)
        if l == 0:
            acc_ref[...] = total
        else:
            acc_ref[...] += pltpu.roll(total, 2 * units * l, 1)
    cols_ref[...] = acc_ref[...].astype(BF16)
    even = parity("lon_2") == 0
    near_ref[...] = jnp.where(even, last_s[...], first_s[...]).astype(BF16)
    far_ref[...] = jnp.where(even, first_s[...], last_s[...]).astype(BF16)


def pack(winds):
    comps, times, levels, rows, lanes = winds.shape
    deep = times // 2 * BIG
    many = levels * comps * times
    edge = jax.ShapeDtypeStruct((many, lanes), BF16)
    return pl.pallas_call(
        pack_kernel,
        in_specs=[pl.BlockSpec(memory_space=pltpu.HBM)],
        out_shape=[
            edge, edge, jax.ShapeDtypeStruct((deep, lanes), BF16), pltpu.VMEM(winds.shape, BF16),
        ],
        scratch_shapes=[
            pltpu.VMEM((many, lanes), F32),
            pltpu.VMEM((many, lanes), F32),
            pltpu.VMEM((deep, lanes), F32),
            pltpu.SemaphoreType.DMA((levels,)),
        ],
        compiler_params=pltpu.CompilerParams(vmem_limit_bytes=16 << 20),
        name="pack",
    )(pltpu.with_memory_space_constraint(winds, pltpu.HBM))


def factors(cos_ref, step_lon, step_lat, shape):
    cos_row = cos_ref[1:2, :]
    by_lon = jnp.broadcast_to(1.0 / (2.0 * step_lon) / cos_row, shape)
    by_up = jnp.broadcast_to(cos_ref[2:3, :] / (2.0 * step_lat) / cos_row, shape)
    by_down = jnp.broadcast_to(cos_ref[0:1, :] / (2.0 * step_lat) / cos_row, shape)
    return by_lon, by_up, by_down


def inner_kernel(step_lon, step_lat, w_ref, cos_ref, g_ref, pick_ref, moved_s):
    comps, times, levels, rows, lanes = w_ref.shape
    groups = rows // SUB
    thirds = rows // BIG
    half = times // 2
    by_lon, by_up, by_down = factors(cos_ref, step_lon, step_lat, (SUB, lanes))
    row = iota((SUB, lanes), 0)
    src = iota((lanes, lanes), 0)
    dst = iota((lanes, lanes), 1)
    shift = jnp.concatenate([as_bf16(src == dst + 1), as_bf16(src == dst - 1)], axis=1)

    wide = pick_ref.shape[1]
    src = iota((lanes, wide), 0)
    dst = iota((lanes, wide), 1)
    at = dst % lanes
    left = dst // lanes * 2
    pick_ref[...] = as_bf16(((at == 0) & (src == left)) | ((at == lanes - 1) & (src == left + 1)))

    @pl.loop(0, levels)
    def _(l):
        for h in range(2):
            for c in range(comps):
                for g in range(thirds):
                    x = w_ref[c, h * half : (h + 1) * half, l, g * BIG : (g + 1) * BIG, :]
                    moved_s[h, c, g] = jnp.dot(
                        x.reshape(half * BIG, lanes), shift, preferred_element_type=F32
                    )
        for t in range(times):
            h = t // half
            by = {}
            for c in range(comps):
                x = w_ref[c, t, l].astype(F32)
                tiles = [x[g * SUB : (g + 1) * SUB] for g in range(groups)]
                up = [pltpu.roll(v, SUB - 1, 0) for v in tiles] + [0.0]
                down = [pltpu.roll(v, 1, 0) for v in tiles] + [0.0]
                for g in range(groups):
                    above = jnp.where(row == SUB - 1, up[g + 1], up[g])
                    below = jnp.where(row == 0, down[g - 1], down[g])
                    at = (t % half) * BIG + g % 2 * SUB
                    east = moved_s[h, c, g // 2, at : at + SUB, :lanes]
                    west = moved_s[h, c, g // 2, at : at + SUB, lanes:]
                    by[c, g] = ((above - below) * by_lon, east * by_up - west * by_down)
            cut = slice(t * SUB, (t + 1) * SUB)
            for g in range(groups):
                g_ref[l, 0, g, cut, :] = by[1, g][0] - by[0, g][1]
                g_ref[l, 1, g, cut, :] = by[0, g][0] + by[1, g][1]


def inner(winds, cos_rows, step_lon, step_lat):
    comps, times, levels, rows, lanes = winds.shape
    groups = rows // SUB
    thirds = rows // BIG
    deep = times * SUB
    whole = pl.BlockSpec(memory_space=pltpu.VMEM)
    elements = winds.size
    return pl.pallas_call(
        functools.partial(inner_kernel, step_lon, step_lat),
        in_specs=[whole] * 2,
        out_specs=[whole] * 2,
        out_shape=[
            jax.ShapeDtypeStruct((levels, 2, groups, deep, lanes), F32),
            jax.ShapeDtypeStruct((lanes, comps * thirds * 2 * lanes), BF16),
        ],
        scratch_shapes=[pltpu.VMEM((2, comps, thirds, times // 2 * BIG, 2 * lanes), F32)],
        compiler_params=pltpu.CompilerParams(vmem_limit_bytes=16 << 20),
        cost_estimate=pl.CostEstimate(
            flops=elements * 4 * lanes, transcendentals=0, bytes_accessed=elements * 6
        ),
        name="inner",
    )(winds, cos_rows)


def outer_kernel(
    step_lon, step_lat, g_ref, pick_ref, near_ref, far_ref, sidea_ref, sideb_ref, cos_ref,
    f_ref, c_ref, prev_s, next_s, halo_s,
):
    levels, _, groups, deep, lanes = g_ref.shape
    times = deep // SUB
    half = times // 2
    thirds = groups // 2
    comps = 2
    units = comps * thirds * 2
    by_lon, by_up, by_down = factors(cos_ref, step_lon, step_lat, (SUB, lanes))
    row = iota((SUB, lanes), 0)
    lane = iota((SUB, lanes), 1)
    by_lat = jnp.where(lane == lanes - 1, by_up, jnp.where(lane == 0, -by_down, 0.0))

    even = parity("lon_2") == 0
    near = near_ref[...].astype(F32)
    far = far_ref[...].astype(F32)
    lon_row = by_lon[0:1, :]
    prev_s[...] = jnp.where(even, far, near) * lon_row
    next_s[...] = jnp.where(even, near, far) * lon_row
    takes = (iota(sidea_ref.shape, 1) + parity("lat")) % 2 == 1
    side = jnp.where(takes, sidea_ref[...].astype(F32), sideb_ref[...].astype(F32))

    def lon_edge(c, t, l, g):
        k = (l * comps + c) * times + t
        if g == 0:
            return jnp.where(row == 0, -prev_s[k : k + 1, :], 0.0)
        if g == groups - 1:
            return jnp.where(row == SUB - 1, next_s[k : k + 1, :], 0.0)
        return None

    def one(t, l):
        h = t // half
        cut = slice(t * SUB, (t + 1) * SUB)
        vort, div = [], []
        for g in range(groups):
            at = (t % half) * BIG + g % 2 * SUB
            lat = []
            for c in range(comps):
                u = unit_of(c, g // 2, h, thirds) * lanes
                lat.append(halo_s[l % 2, at : at + SUB, u : u + lanes] * by_lat)
            first = g_ref[l, 0, g, cut, :] - lat[0]
            second = g_ref[l, 1, g, cut, :] + lat[1]
            if g in (0, groups - 1):
                first = first + lon_edge(1, t, l, g)
                second = second + lon_edge(0, t, l, g)
            vort.append(first)
            div.append(second)
        return vort, div

    total = None
    for l in range(levels):
        mine = side if l == 0 else pltpu.roll(side, lanes - 2 * units * l, 1)
        halo_s[l % 2] = jnp.dot(mine.astype(BF16), pick_ref[...], preferred_element_type=F32)
        for pair in range(times // 2):
            early, late = one(2 * pair, l), one(2 * pair + 1, l)
            at = pair * 2 * SUB
            for s in range(2):
                for g in range(groups):
                    both = jnp.concatenate([early[s][g], late[s][g]], axis=0)
                    f_ref[l, s, g, at : at + 2 * SUB, :] = both.astype(BF16)
        for s in range(2):
            x = jnp.concatenate([f_ref[l, s, g] for g in range(groups)], axis=1)
            term = lax.dot_general(x, x, (((1,), (1,)), ((), ())), preferred_element_type=F32)
            total = term if total is None else total + term

    same = iota((deep, deep), 0) % SUB == iota((deep, deep), 1) % SUB
    kept = jnp.where(same, total, 0.0)
    kept = kept.reshape(times, SUB, deep).sum(axis=1)
    fold = as_bf16(iota((deep, times), 0) // SUB == iota((deep, times), 1))
    cov = jnp.dot(
        jnp.concatenate(three_terms(kept), axis=1),
        jnp.concatenate([fold] * 3, axis=0),
        preferred_element_type=F32,
    )
    c_ref[...] = jnp.concatenate([cov[q * SUB : (q + 1) * SUB] for q in range(times // SUB)], axis=1)


def outer(g, pick, near, far, sidea, sideb, cos_rows, step_lon, step_lat):
    lanes = g.shape[-1]
    whole = pl.BlockSpec(memory_space=pltpu.VMEM)
    return pl.pallas_call(
        functools.partial(outer_kernel, step_lon, step_lat),
        in_specs=[whole] * 7,
        out_specs=[whole, whole],
        out_shape=[pltpu.VMEM(g.shape, BF16), jax.ShapeDtypeStruct((SUB, lanes), F32)],
        scratch_shapes=[
            pltpu.VMEM(near.shape, F32),
            pltpu.VMEM(near.shape, F32),
            pltpu.VMEM((2, sidea.shape[0], pick.shape[1]), F32),
        ],
        compiler_params=pltpu.CompilerParams(vmem_limit_bytes=16 << 20),
        name="outer",
    )(g, pick, near, far, sidea, sideb, cos_rows)


def transform(cov, table, total_rows, lanes):
    times = table.shape[1]
    half = lanes // 2
    table_b = table.astype(BF16)
    left = jnp.dot(
        jnp.concatenate([table_b] * 3, axis=1),
        jnp.concatenate(three_terms(cov), axis=0),
        preferred_element_type=F32,
    )
    gram = lax.dot_general(
        jnp.concatenate(three_terms(left), axis=1),
        jnp.concatenate([table_b] * 3, axis=1),
        (((1,), (1,)), ((), ())),
        preferred_element_type=F32,
    ) / total_rows
    row = iota((COLS, lanes), 0)
    lane = iota((COLS, lanes), 1)
    near = lane < half
    pad = jnp.zeros((COLS, half - COLS - times), F32)
    parts, sizes = [], []
    for f in range(FREQS):
        at = slice(f * COLS, (f + 1) * COLS)
        own = gram[at, at]
        diagonal = iota((COLS, COLS), 0) == iota((COLS, COLS), 1)
        size = jnp.max(jnp.where(diagonal, own, 0.0), axis=(0, 1), keepdims=True)
        sizes.append(size)
        parts += [own / size, table[at], pad]
    a = jnp.concatenate(parts, axis=1)

    for j in range(0, COLS, 2):
        c1 = jnp.where(near, a[:, j : j + 1], a[:, half + j : half + j + 1])
        c2 = jnp.where(near, a[:, j + 1 : j + 2], a[:, half + j + 1 : half + j + 2])
        r1 = a[j : j + 1, :]
        r2 = a[j + 1 : j + 2, :]
        p11 = c1[j : j + 1]
        p12 = c2[j : j + 1]
        p22 = c2[j + 1 : j + 2]
        inverse = 1.0 / (p11 * p22 - p12 * p12)
        s1 = (p22 * r1 - p12 * r2) * inverse
        s2 = (p11 * r2 - p12 * r1) * inverse
        a = jnp.where(row > j + 1, a - c1 * s1 - c2 * s2, a)

    odd = iota((COLS, 1), 0) % 2 == 1
    weights = []
    before = pltpu.roll(a, 1, 0)
    for f in range(FREQS):
        base = f * half
        on = jnp.sum(jnp.where(lane == base + row, a, 0.0), axis=1, keepdims=True)
        off = jnp.sum(jnp.where(lane == base + row - 1, a, 0.0), axis=1, keepdims=True)
        above = jnp.sum(jnp.where(lane == base + row - 1, before, 0.0), axis=1, keepdims=True)
        ratio = jnp.where(odd, off / above, 0.0)
        pivot = on - ratio * off
        cut = slice(base + COLS, base + COLS + times)
        weights.append((a[:, cut] - ratio * before[:, cut]) / jnp.sqrt(pivot) / jnp.sqrt(sizes[f]))
    return jnp.concatenate(weights, axis=0)


def basis_kernel(total_rows, sums_ref, table_ref, f_ref, out_hbm, out_ref, mix_ref, sems):
    levels, kinds, groups, deep, lanes = f_ref.shape
    times = deep // SUB
    outs = FREQS * COLS
    flat = jnp.sum(sums_ref[...], axis=0)
    cov = jnp.concatenate([flat[:, q * times : (q + 1) * times] for q in range(times // SUB)], axis=0)
    w = transform(cov, table_ref[...], total_rows, lanes)
    w_hi = w.astype(BF16)
    w_lo = (w - w_hi.astype(F32)).astype(BF16)
    spread = as_bf16(iota((outs * SUB, outs), 0) // SUB == iota((outs * SUB, outs), 1))
    widen = as_bf16(iota((times, deep), 0) == iota((times, deep), 1) // SUB)
    same = iota((outs * SUB, deep), 0) % SUB == iota((outs * SUB, deep), 1) % SUB
    for k, term in enumerate((w_hi, w_lo)):
        tall = jnp.dot(spread, term, preferred_element_type=F32).astype(BF16)
        full = jnp.dot(tall, widen, preferred_element_type=F32)
        mix_ref[:, k * deep : (k + 1) * deep] = jnp.where(same, full, 0.0).astype(BF16)

    @pl.loop(0, levels)
    def _(l):
        for s in range(kinds):
            for g in range(0, groups, 2):
                x = jnp.concatenate([f_ref[l, s, g], f_ref[l, s, g + 1]], axis=1)
                x = jnp.concatenate([x, x], axis=0)
                y = jnp.dot(mix_ref[...], x, preferred_element_type=F32)
                for e in range(2):
                    part = y[:, e * lanes : (e + 1) * lanes].reshape(outs, SUB, lanes)
                    out_ref[:, s, l, (g + e) * SUB : (g + e + 1) * SUB, :] = part
            pltpu.make_async_copy(out_ref.at[:, s, l], out_hbm.at[:, s, l], sems.at[s, l]).start()

    for l in range(levels):
        for s in range(kinds):
            pltpu.make_async_copy(out_ref.at[:, s, l], out_hbm.at[:, s, l], sems.at[s, l]).wait()


def basis_of(sums, table, f, total_rows):
    levels, kinds, groups, deep, lanes = f.shape
    outs = FREQS * COLS
    whole = pl.BlockSpec(memory_space=pltpu.VMEM)
    out_shape = (outs, kinds, levels, groups * SUB, lanes)
    return pl.pallas_call(
        functools.partial(basis_kernel, total_rows),
        in_specs=[whole, whole, whole],
        out_specs=pl.BlockSpec(memory_space=pltpu.HBM),
        out_shape=pltpu.HBM(out_shape, F32),
        scratch_shapes=[
            pltpu.VMEM(out_shape, F32),
            pltpu.VMEM((outs * SUB, 2 * deep), BF16),
            pltpu.SemaphoreType.DMA((kinds, levels)),
        ],
        compiler_params=pltpu.CompilerParams(vmem_limit_bytes=16 << 20),
        name="basis",
    )(sums, table, f)


def exchange(x, axes):
    copies = jnp.broadcast_to(x, (lax.axis_size(axes), *x.shape))
    return lax.all_to_all(copies, axes, split_axis=0, concat_axis=0, tiled=True)


def swap(x, axes, offset):
    size = lax.axis_size(axes)
    pairs = []
    for i in range(offset, size, 2):
        pairs += [(i, (i + 1) % size), ((i + 1) % size, i)]
    return lax.ppermute(x, axes, pairs)


def body(winds):
    _, times, levels, lon_cells, lat_cells = winds.shape
    grid_lon = lon_cells * lax.axis_size(LON)
    grid_lat = lat_cells * lax.axis_size("lat")
    step_lon = 2.0 * math.pi / grid_lon
    step_lat = 2.6 / grid_lat
    near, far, cols, winds = pack(winds)
    near = swap(near, "lon_2", 0)
    far = swap(far, LON, 1)
    sidea = swap(cols, "lat", 0)
    sideb = swap(cols, "lat", 1)
    shape = (SUB, lat_cells)
    index = lax.axis_index("lat") * lat_cells + iota(shape, 1) + iota(shape, 0) - 1
    inside = (index >= 0) & (index < grid_lat)
    cos_rows = jnp.where(inside, jnp.cos(-1.3 + (index.astype(F32) + 0.5) * step_lat), 0.0)
    g, pick = inner(winds, cos_rows, step_lon, step_lat)
    f, cov = outer(g, pick, near, far, sidea, sideb, cos_rows, step_lon, step_lat)
    half_sums = exchange(cov, ("lon_2", "lat")).sum(axis=0)
    sums = exchange(half_sums, ("lon_0", "lon_1"))
    return basis_of(sums, jnp.asarray(taper_table()), f, 2 * levels * grid_lon * grid_lat)


def solution(mesh):
    split = Mesh(
        mesh.devices.reshape(4, 4, 2, mesh.shape["lat"]), ("lon_0", "lon_1", "lon_2", "lat")
    )
    placed = (P(None, None, None, LON, "lat"),)
    return jax.shard_map(
        body,
        mesh=split,
        in_specs=placed,
        out_specs=P(None, None, None, LON, "lat"),
        check_vma=False,
    )
```

```python
import functools
import math

import jax
import jax.numpy as jnp
import numpy as np
from jax import lax
from jax.experimental import pallas as pl
from jax.experimental.pallas import tpu as pltpu
from jax.sharding import Mesh
from jax.sharding import PartitionSpec as P

TIME = 32
TAPERS = 12
FREQS = 2
COLS = 2 * TAPERS
LON = ("lon_0", "lon_1", "lon_2")
SUB = 8
BIG = 16
F32 = jnp.float32
BF16 = jnp.bfloat16


def taper_table():
    t = np.arange(TIME, dtype=np.float32)
    k = np.arange(TAPERS, dtype=np.float32)
    weights = np.float32(math.sqrt(2.0 / (TIME + 1))) * np.sin(
        np.float32(math.pi)
        * (k[:, None] + np.float32(1.0))
        * (t[None, :] + np.float32(1.0))
        / np.float32(TIME + 1)
    )
    blocks = []
    for which in range(FREQS):
        phases = np.float32(2.0 * math.pi * (7 + 2 * which)) * t / np.float32(TIME)
        real_part = weights * np.cos(phases)[None, :]
        imag_part = -weights * np.sin(phases)[None, :]
        blocks.append(np.stack([real_part, imag_part], axis=1).reshape(COLS, TIME))
    return np.concatenate(blocks, axis=0).astype(jnp.bfloat16).astype(np.float32)


def iota(shape, dim):
    return lax.broadcasted_iota(jnp.int32, shape, dim)


def parity(axis):
    return lax.axis_index(axis) % 2


def as_bf16(mask):
    return mask.astype(F32).astype(BF16)


def three_terms(x):
    first = x.astype(BF16)
    rest = x - first.astype(F32)
    second = rest.astype(BF16)
    third = (rest - second.astype(F32)).astype(BF16)
    return first, second, third


def unit_of(c, g, h, thirds):
    return (c * thirds + g) * 2 + h


def pack_kernel(
    w_hbm, near_ref, far_ref, cols_ref, w_ref, first_s, last_s, acc_ref, sems,
):
    comps, times, levels, rows, lanes = w_ref.shape
    half = times // 2
    thirds = rows // BIG
    units = comps * thirds * 2
    copies = {}
    for l in range(levels):
        for h in range(2):
            cut = pl.ds(h * half, half)
            copies[l, h] = pltpu.make_async_copy(
                w_hbm.at[:, cut, l], w_ref.at[:, cut, l], sems.at[l, h]
            )
            copies[l, h].start()
    deep = half * BIG
    chunk = comps * thirds
    at = iota((chunk * lanes, lanes), 0)
    spot = iota((chunk * lanes, lanes), 1)
    here = at % lanes
    want = at // lanes * 4
    hits = []
    for h in range(2):
        lower = want + 2 * h
        hits.append(as_bf16(((here == lanes - 1) & (spot == lower)) | ((here == 0) & (spot == lower + 1))))
    for l in range(levels):
        total = None
        for h in range(2):
            copies[l, h].wait()
            pieces = []
            for c in range(comps):
                for g in range(thirds):
                    x = w_ref[c, h * half : (h + 1) * half, l, g * BIG : (g + 1) * BIG, :]
                    pieces.append(x.reshape(deep, lanes))
                for t in range(h * half, (h + 1) * half):
                    k = (l * comps + c) * times + t
                    first_s[k : k + 1, :] = w_ref[c, t, l, 0:BIG, :].astype(F32)[0:1]
                    last_s[k : k + 1, :] = w_ref[c, t, l, rows - BIG : rows, :].astype(F32)[BIG - 1 : BIG]
            term = jnp.dot(jnp.concatenate(pieces, axis=1), hits[h], preferred_element_type=F32)
            total = term if total is None else total + term
        if l == 0:
            acc_ref[...] = total
        else:
            acc_ref[...] += pltpu.roll(total, 2 * units * l, 1)
    cols_ref[...] = acc_ref[...].astype(BF16)
    even = parity("lon_2") == 0
    near_ref[...] = jnp.where(even, last_s[...], first_s[...]).astype(BF16)
    far_ref[...] = jnp.where(even, first_s[...], last_s[...]).astype(BF16)


def pack(winds):
    comps, times, levels, rows, lanes = winds.shape
    deep = times // 2 * BIG
    many = levels * comps * times
    edge = jax.ShapeDtypeStruct((many, lanes), BF16)
    return pl.pallas_call(
        pack_kernel,
        in_specs=[pl.BlockSpec(memory_space=pltpu.HBM)],
        out_shape=[
            edge, edge, jax.ShapeDtypeStruct((deep, lanes), BF16), pltpu.VMEM(winds.shape, BF16),
        ],
        scratch_shapes=[
            pltpu.VMEM((many, lanes), F32),
            pltpu.VMEM((many, lanes), F32),
            pltpu.VMEM((deep, lanes), F32),
            pltpu.SemaphoreType.DMA((levels, 2)),
        ],
        compiler_params=pltpu.CompilerParams(vmem_limit_bytes=16 << 20),
        name="pack",
    )(pltpu.with_memory_space_constraint(winds, pltpu.HBM))


def factors(cos_ref, step_lon, step_lat, shape):
    cos_row = cos_ref[1:2, :]
    by_lon = jnp.broadcast_to(1.0 / (2.0 * step_lon) / cos_row, shape)
    by_up = jnp.broadcast_to(cos_ref[2:3, :] / (2.0 * step_lat) / cos_row, shape)
    by_down = jnp.broadcast_to(cos_ref[0:1, :] / (2.0 * step_lat) / cos_row, shape)
    return by_lon, by_up, by_down


def inner_kernel(step_lon, step_lat, w_ref, cos_ref, g_ref, pick_ref, moved_s):
    comps, times, levels, rows, lanes = w_ref.shape
    groups = rows // SUB
    thirds = rows // BIG
    half = times // 2
    by_lon, by_up, by_down = factors(cos_ref, step_lon, step_lat, (SUB, lanes))
    row = iota((SUB, lanes), 0)
    src = iota((lanes, lanes), 0)
    dst = iota((lanes, lanes), 1)
    shift = jnp.concatenate([as_bf16(src == dst + 1), as_bf16(src == dst - 1)], axis=1)

    wide = pick_ref.shape[1]
    src = iota((lanes, wide), 0)
    dst = iota((lanes, wide), 1)
    at = dst % lanes
    left = dst // lanes * 2
    pick_ref[...] = as_bf16(((at == 0) & (src == left)) | ((at == lanes - 1) & (src == left + 1)))

    @pl.loop(0, levels)
    def _(l):
        for h in range(2):
            for c in range(comps):
                for g in range(thirds):
                    x = w_ref[c, h * half : (h + 1) * half, l, g * BIG : (g + 1) * BIG, :]
                    moved_s[h, c, g] = jnp.dot(
                        x.reshape(half * BIG, lanes), shift, preferred_element_type=F32
                    )
        for t in range(times):
            h = t // half
            by = {}
            for c in range(comps):
                x = w_ref[c, t, l].astype(F32)
                tiles = [x[g * SUB : (g + 1) * SUB] for g in range(groups)]
                up = [pltpu.roll(v, SUB - 1, 0) for v in tiles] + [0.0]
                down = [pltpu.roll(v, 1, 0) for v in tiles] + [0.0]
                for g in range(groups):
                    above = jnp.where(row == SUB - 1, up[g + 1], up[g])
                    below = jnp.where(row == 0, down[g - 1], down[g])
                    at = (t % half) * BIG + g % 2 * SUB
                    east = moved_s[h, c, g // 2, at : at + SUB, :lanes]
                    west = moved_s[h, c, g // 2, at : at + SUB, lanes:]
                    by[c, g] = ((above - below) * by_lon, east * by_up - west * by_down)
            cut = slice(t * SUB, (t + 1) * SUB)
            for g in range(groups):
                g_ref[l, 0, g, cut, :] = by[1, g][0] - by[0, g][1]
                g_ref[l, 1, g, cut, :] = by[0, g][0] + by[1, g][1]


def inner(winds, cos_rows, step_lon, step_lat):
    comps, times, levels, rows, lanes = winds.shape
    groups = rows // SUB
    thirds = rows // BIG
    deep = times * SUB
    whole = pl.BlockSpec(memory_space=pltpu.VMEM)
    elements = winds.size
    return pl.pallas_call(
        functools.partial(inner_kernel, step_lon, step_lat),
        in_specs=[whole] * 2,
        out_specs=[whole] * 2,
        out_shape=[
            jax.ShapeDtypeStruct((levels, 2, groups, deep, lanes), F32),
            jax.ShapeDtypeStruct((lanes, comps * thirds * 2 * lanes), BF16),
        ],
        scratch_shapes=[pltpu.VMEM((2, comps, thirds, times // 2 * BIG, 2 * lanes), F32)],
        compiler_params=pltpu.CompilerParams(vmem_limit_bytes=16 << 20),
        cost_estimate=pl.CostEstimate(
            flops=elements * 4 * lanes, transcendentals=0, bytes_accessed=elements * 6
        ),
        name="inner",
    )(winds, cos_rows)


def outer_kernel(
    step_lon, step_lat, g_ref, pick_ref, near_ref, far_ref, sidea_ref, sideb_ref, cos_ref,
    f_ref, c_ref, prev_s, next_s, halo_s,
):
    levels, _, groups, deep, lanes = g_ref.shape
    times = deep // SUB
    half = times // 2
    thirds = groups // 2
    comps = 2
    units = comps * thirds * 2
    by_lon, by_up, by_down = factors(cos_ref, step_lon, step_lat, (SUB, lanes))
    row = iota((SUB, lanes), 0)
    lane = iota((SUB, lanes), 1)
    by_lat = jnp.where(lane == lanes - 1, by_up, jnp.where(lane == 0, -by_down, 0.0))

    even = parity("lon_2") == 0
    near = near_ref[...].astype(F32)
    far = far_ref[...].astype(F32)
    lon_row = by_lon[0:1, :]
    prev_s[...] = jnp.where(even, far, near) * lon_row
    next_s[...] = jnp.where(even, near, far) * lon_row
    takes = (iota(sidea_ref.shape, 1) + parity("lat")) % 2 == 1
    side = jnp.where(takes, sidea_ref[...].astype(F32), sideb_ref[...].astype(F32))

    def lon_edge(c, t, l, g):
        k = (l * comps + c) * times + t
        if g == 0:
            return jnp.where(row == 0, -prev_s[k : k + 1, :], 0.0)
        if g == groups - 1:
            return jnp.where(row == SUB - 1, next_s[k : k + 1, :], 0.0)
        return None

    def one(t, l):
        h = t // half
        cut = slice(t * SUB, (t + 1) * SUB)
        vort, div = [], []
        for g in range(groups):
            at = (t % half) * BIG + g % 2 * SUB
            lat = []
            for c in range(comps):
                u = unit_of(c, g // 2, h, thirds) * lanes
                lat.append(halo_s[l % 2, at : at + SUB, u : u + lanes] * by_lat)
            first = g_ref[l, 0, g, cut, :] - lat[0]
            second = g_ref[l, 1, g, cut, :] + lat[1]
            if g in (0, groups - 1):
                first = first + lon_edge(1, t, l, g)
                second = second + lon_edge(0, t, l, g)
            vort.append(first)
            div.append(second)
        return vort, div

    total = None
    for l in range(levels):
        mine = side if l == 0 else pltpu.roll(side, lanes - 2 * units * l, 1)
        halo_s[l % 2] = jnp.dot(mine.astype(BF16), pick_ref[...], preferred_element_type=F32)
        for pair in range(times // 2):
            early, late = one(2 * pair, l), one(2 * pair + 1, l)
            at = pair * 2 * SUB
            for s in range(2):
                for g in range(groups):
                    both = jnp.concatenate([early[s][g], late[s][g]], axis=0)
                    f_ref[l, s, g, at : at + 2 * SUB, :] = both.astype(BF16)
        for s in range(2):
            x = jnp.concatenate([f_ref[l, s, g] for g in range(groups)], axis=1)
            term = lax.dot_general(x, x, (((1,), (1,)), ((), ())), preferred_element_type=F32)
            total = term if total is None else total + term

    same = iota((deep, deep), 0) % SUB == iota((deep, deep), 1) % SUB
    kept = jnp.where(same, total, 0.0)
    kept = kept.reshape(times, SUB, deep).sum(axis=1)
    fold = as_bf16(iota((deep, times), 0) // SUB == iota((deep, times), 1))
    cov = jnp.dot(
        jnp.concatenate(three_terms(kept), axis=1),
        jnp.concatenate([fold] * 3, axis=0),
        preferred_element_type=F32,
    )
    c_ref[...] = jnp.concatenate([cov[q * SUB : (q + 1) * SUB] for q in range(times // SUB)], axis=1)


def outer(g, pick, near, far, sidea, sideb, cos_rows, step_lon, step_lat):
    lanes = g.shape[-1]
    whole = pl.BlockSpec(memory_space=pltpu.VMEM)
    return pl.pallas_call(
        functools.partial(outer_kernel, step_lon, step_lat),
        in_specs=[whole] * 7,
        out_specs=[whole, whole],
        out_shape=[pltpu.VMEM(g.shape, BF16), jax.ShapeDtypeStruct((SUB, lanes), F32)],
        scratch_shapes=[
            pltpu.VMEM(near.shape, F32),
            pltpu.VMEM(near.shape, F32),
            pltpu.VMEM((2, sidea.shape[0], pick.shape[1]), F32),
        ],
        compiler_params=pltpu.CompilerParams(vmem_limit_bytes=16 << 20),
        name="outer",
    )(g, pick, near, far, sidea, sideb, cos_rows)


def transform(cov, table, total_rows, lanes):
    times = table.shape[1]
    half = lanes // 2
    table_b = table.astype(BF16)
    left = jnp.dot(
        jnp.concatenate([table_b] * 3, axis=1),
        jnp.concatenate(three_terms(cov), axis=0),
        preferred_element_type=F32,
    )
    gram = lax.dot_general(
        jnp.concatenate(three_terms(left), axis=1),
        jnp.concatenate([table_b] * 3, axis=1),
        (((1,), (1,)), ((), ())),
        preferred_element_type=F32,
    ) / total_rows
    row = iota((COLS, lanes), 0)
    lane = iota((COLS, lanes), 1)
    near = lane < half
    pad = jnp.zeros((COLS, half - COLS - times), F32)
    parts, sizes = [], []
    for f in range(FREQS):
        at = slice(f * COLS, (f + 1) * COLS)
        own = gram[at, at]
        diagonal = iota((COLS, COLS), 0) == iota((COLS, COLS), 1)
        size = jnp.max(jnp.where(diagonal, own, 0.0), axis=(0, 1), keepdims=True)
        sizes.append(size)
        parts += [own / size, table[at], pad]
    a = jnp.concatenate(parts, axis=1)

    for j in range(0, COLS, 2):
        c1 = jnp.where(near, a[:, j : j + 1], a[:, half + j : half + j + 1])
        c2 = jnp.where(near, a[:, j + 1 : j + 2], a[:, half + j + 1 : half + j + 2])
        r1 = a[j : j + 1, :]
        r2 = a[j + 1 : j + 2, :]
        p11 = c1[j : j + 1]
        p12 = c2[j : j + 1]
        p22 = c2[j + 1 : j + 2]
        inverse = 1.0 / (p11 * p22 - p12 * p12)
        s1 = (p22 * r1 - p12 * r2) * inverse
        s2 = (p11 * r2 - p12 * r1) * inverse
        a = jnp.where(row > j + 1, a - c1 * s1 - c2 * s2, a)

    odd = iota((COLS, 1), 0) % 2 == 1
    weights = []
    before = pltpu.roll(a, 1, 0)
    for f in range(FREQS):
        base = f * half
        on = jnp.sum(jnp.where(lane == base + row, a, 0.0), axis=1, keepdims=True)
        off = jnp.sum(jnp.where(lane == base + row - 1, a, 0.0), axis=1, keepdims=True)
        above = jnp.sum(jnp.where(lane == base + row - 1, before, 0.0), axis=1, keepdims=True)
        ratio = jnp.where(odd, off / above, 0.0)
        pivot = on - ratio * off
        cut = slice(base + COLS, base + COLS + times)
        weights.append((a[:, cut] - ratio * before[:, cut]) / jnp.sqrt(pivot) / jnp.sqrt(sizes[f]))
    return jnp.concatenate(weights, axis=0)


def basis_kernel(total_rows, sums_ref, table_ref, f_ref, out_hbm, out_ref, mix_ref, sems):
    levels, kinds, groups, deep, lanes = f_ref.shape
    times = deep // SUB
    outs = FREQS * COLS
    flat = jnp.sum(sums_ref[...], axis=0)
    cov = jnp.concatenate([flat[:, q * times : (q + 1) * times] for q in range(times // SUB)], axis=0)
    w = transform(cov, table_ref[...], total_rows, lanes)
    w_hi = w.astype(BF16)
    w_lo = (w - w_hi.astype(F32)).astype(BF16)
    spread = as_bf16(iota((outs * SUB, outs), 0) // SUB == iota((outs * SUB, outs), 1))
    widen = as_bf16(iota((times, deep), 0) == iota((times, deep), 1) // SUB)
    same = iota((outs * SUB, deep), 0) % SUB == iota((outs * SUB, deep), 1) % SUB
    for k, term in enumerate((w_hi, w_lo)):
        tall = jnp.dot(spread, term, preferred_element_type=F32).astype(BF16)
        full = jnp.dot(tall, widen, preferred_element_type=F32)
        mix_ref[:, k * deep : (k + 1) * deep] = jnp.where(same, full, 0.0).astype(BF16)

    @pl.loop(0, levels)
    def _(l):
        for s in range(kinds):
            for g in range(0, groups, 2):
                x = jnp.concatenate([f_ref[l, s, g], f_ref[l, s, g + 1]], axis=1)
                x = jnp.concatenate([x, x], axis=0)
                y = jnp.dot(mix_ref[...], x, preferred_element_type=F32)
                for e in range(2):
                    part = y[:, e * lanes : (e + 1) * lanes].reshape(outs, SUB, lanes)
                    out_ref[:, s, l, (g + e) * SUB : (g + e + 1) * SUB, :] = part
            pltpu.make_async_copy(out_ref.at[:, s, l], out_hbm.at[:, s, l], sems.at[s, l]).start()

    for l in range(levels):
        for s in range(kinds):
            pltpu.make_async_copy(out_ref.at[:, s, l], out_hbm.at[:, s, l], sems.at[s, l]).wait()


def basis_of(sums, table, f, total_rows):
    levels, kinds, groups, deep, lanes = f.shape
    outs = FREQS * COLS
    whole = pl.BlockSpec(memory_space=pltpu.VMEM)
    out_shape = (outs, kinds, levels, groups * SUB, lanes)
    return pl.pallas_call(
        functools.partial(basis_kernel, total_rows),
        in_specs=[whole, whole, whole],
        out_specs=pl.BlockSpec(memory_space=pltpu.HBM),
        out_shape=pltpu.HBM(out_shape, F32),
        scratch_shapes=[
            pltpu.VMEM(out_shape, F32),
            pltpu.VMEM((outs * SUB, 2 * deep), BF16),
            pltpu.SemaphoreType.DMA((kinds, levels)),
        ],
        compiler_params=pltpu.CompilerParams(vmem_limit_bytes=16 << 20),
        name="basis",
    )(sums, table, f)


def exchange(x, axes):
    copies = jnp.broadcast_to(x, (lax.axis_size(axes), *x.shape))
    return lax.all_to_all(copies, axes, split_axis=0, concat_axis=0, tiled=True)


def swap(x, axes, offset, around=True):
    size = lax.axis_size(axes)
    pairs = []
    for i in range(offset, size if around else size - 1, 2):
        pairs += [(i, (i + 1) % size), ((i + 1) % size, i)]
    return lax.ppermute(x, axes, pairs)


def body(winds):
    _, times, levels, lon_cells, lat_cells = winds.shape
    grid_lon = lon_cells * lax.axis_size(LON)
    grid_lat = lat_cells * lax.axis_size("lat")
    step_lon = 2.0 * math.pi / grid_lon
    step_lat = 2.6 / grid_lat
    near, far, cols, winds = pack(winds)
    near = swap(near, "lon_2", 0)
    far = swap(far, LON, 1)
    sidea = swap(cols, "lat", 0)
    sideb = swap(cols, "lat", 1, around=False)
    shape = (SUB, lat_cells)
    index = lax.axis_index("lat") * lat_cells + iota(shape, 1) + iota(shape, 0) - 1
    inside = (index >= 0) & (index < grid_lat)
    cos_rows = jnp.where(inside, jnp.cos(-1.3 + (index.astype(F32) + 0.5) * step_lat), 0.0)
    g, pick = inner(winds, cos_rows, step_lon, step_lat)
    f, cov = outer(g, pick, near, far, sidea, sideb, cos_rows, step_lon, step_lat)
    half_sums = exchange(cov, ("lon_2", "lat")).sum(axis=0)
    sums = exchange(half_sums, ("lon_0", "lon_1"))
    return basis_of(sums, jnp.asarray(taper_table()), f, 2 * levels * grid_lon * grid_lat)


def solution(mesh):
    split = Mesh(
        mesh.devices.reshape(4, 4, 2, mesh.shape["lat"]), ("lon_0", "lon_1", "lon_2", "lat")
    )
    placed = (P(None, None, None, LON, "lat"),)
    return jax.shard_map(
        body,
        mesh=split,
        in_specs=placed,
        out_specs=P(None, None, None, LON, "lat"),
        check_vma=False,
    )
```

```python
import functools
import math

import jax
import jax.numpy as jnp
import numpy as np
from jax import lax
from jax.experimental import pallas as pl
from jax.experimental.pallas import tpu as pltpu
from jax.sharding import Mesh
from jax.sharding import PartitionSpec as P

TIME = 32
TAPERS = 12
FREQS = 2
COLS = 2 * TAPERS
LON = ("lon_0", "lon_1", "lon_2")
SUB = 8
BIG = 16
F32 = jnp.float32
BF16 = jnp.bfloat16


def taper_table():
    t = np.arange(TIME, dtype=np.float32)
    k = np.arange(TAPERS, dtype=np.float32)
    weights = np.float32(math.sqrt(2.0 / (TIME + 1))) * np.sin(
        np.float32(math.pi)
        * (k[:, None] + np.float32(1.0))
        * (t[None, :] + np.float32(1.0))
        / np.float32(TIME + 1)
    )
    blocks = []
    for which in range(FREQS):
        phases = np.float32(2.0 * math.pi * (7 + 2 * which)) * t / np.float32(TIME)
        real_part = weights * np.cos(phases)[None, :]
        imag_part = -weights * np.sin(phases)[None, :]
        blocks.append(np.stack([real_part, imag_part], axis=1).reshape(COLS, TIME))
    return np.concatenate(blocks, axis=0).astype(jnp.bfloat16).astype(np.float32)


def iota(shape, dim):
    return lax.broadcasted_iota(jnp.int32, shape, dim)


def parity(axis):
    return lax.axis_index(axis) % 2


def as_bf16(mask):
    return mask.astype(F32).astype(BF16)


def three_terms(x):
    first = x.astype(BF16)
    rest = x - first.astype(F32)
    second = rest.astype(BF16)
    third = (rest - second.astype(F32)).astype(BF16)
    return first, second, third


def unit_of(c, g, h, thirds):
    return (c * thirds + g) * 2 + h


def pack_kernel(
    w_hbm, near_ref, far_ref, cols_ref, w_ref, first_s, last_s, acc_ref, sems,
):
    comps, times, levels, rows, lanes = w_ref.shape
    half = times // 2
    thirds = rows // BIG
    units = comps * thirds * 2
    copies = [
        pltpu.make_async_copy(w_hbm.at[:, :, l], w_ref.at[:, :, l], sems.at[l]) for l in range(levels)
    ]
    for copy in copies:
        copy.start()
    deep = half * BIG
    at = iota((units * lanes, lanes), 0)
    spot = iota((units * lanes, lanes), 1)
    here = at % lanes
    want = at // lanes * 2
    hit = as_bf16(((here == lanes - 1) & (spot == want)) | ((here == 0) & (spot == want + 1)))
    for l in range(levels):
        copies[l].wait()
        pieces = []
        for c in range(comps):
            for g in range(thirds):
                for h in range(2):
                    x = w_ref[c, h * half : (h + 1) * half, l, g * BIG : (g + 1) * BIG, :]
                    pieces.append(x.reshape(deep, lanes))
            for t in range(times):
                k = (l * comps + c) * times + t
                first_s[k : k + 1, :] = w_ref[c, t, l, 0:BIG, :].astype(F32)[0:1]
                last_s[k : k + 1, :] = w_ref[c, t, l, rows - BIG : rows, :].astype(F32)[BIG - 1 : BIG]
        total = jnp.dot(jnp.concatenate(pieces, axis=1), hit, preferred_element_type=F32)
        if l == 0:
            acc_ref[...] = total
        else:
            acc_ref[...] += pltpu.roll(total, 2 * units * l, 1)
    cols_ref[...] = acc_ref[...].astype(BF16)
    even = parity("lon_2") == 0
    near_ref[...] = jnp.where(even, last_s[...], first_s[...]).astype(BF16)
    far_ref[...] = jnp.where(even, first_s[...], last_s[...]).astype(BF16)


def pack(winds):
    comps, times, levels, rows, lanes = winds.shape
    deep = times // 2 * BIG
    many = levels * comps * times
    edge = jax.ShapeDtypeStruct((many, lanes), BF16)
    return pl.pallas_call(
        pack_kernel,
        in_specs=[pl.BlockSpec(memory_space=pltpu.HBM)],
        out_shape=[
            edge, edge, jax.ShapeDtypeStruct((deep, lanes), BF16), pltpu.VMEM(winds.shape, BF16),
        ],
        scratch_shapes=[
            pltpu.VMEM((many, lanes), F32),
            pltpu.VMEM((many, lanes), F32),
            pltpu.VMEM((deep, lanes), F32),
            pltpu.SemaphoreType.DMA((levels,)),
        ],
        compiler_params=pltpu.CompilerParams(vmem_limit_bytes=16 << 20),
        name="pack",
    )(pltpu.with_memory_space_constraint(winds, pltpu.HBM))


def factors(cos_ref, step_lon, step_lat, shape):
    cos_row = cos_ref[1:2, :]
    by_lon = jnp.broadcast_to(1.0 / (2.0 * step_lon) / cos_row, shape)
    by_up = jnp.broadcast_to(cos_ref[2:3, :] / (2.0 * step_lat) / cos_row, shape)
    by_down = jnp.broadcast_to(cos_ref[0:1, :] / (2.0 * step_lat) / cos_row, shape)
    return by_lon, by_up, by_down


def inner_kernel(step_lon, step_lat, w_ref, cos_ref, g_ref, pick_ref, moved_s):
    comps, times, levels, rows, lanes = w_ref.shape
    groups = rows // SUB
    thirds = rows // BIG
    half = times // 2
    by_lon, by_up, by_down = factors(cos_ref, step_lon, step_lat, (SUB, lanes))
    row = iota((SUB, lanes), 0)
    src = iota((lanes, lanes), 0)
    dst = iota((lanes, lanes), 1)
    shift = jnp.concatenate([as_bf16(src == dst + 1), as_bf16(src == dst - 1)], axis=1)

    wide = pick_ref.shape[1]
    src = iota((lanes, wide), 0)
    dst = iota((lanes, wide), 1)
    at = dst % lanes
    left = dst // lanes * 2
    pick_ref[...] = as_bf16(((at == 0) & (src == left)) | ((at == lanes - 1) & (src == left + 1)))

    @pl.loop(0, levels)
    def _(l):
        for h in range(2):
            for c in range(comps):
                for g in range(thirds):
                    x = w_ref[c, h * half : (h + 1) * half, l, g * BIG : (g + 1) * BIG, :]
                    moved_s[h, c, g] = jnp.dot(
                        x.reshape(half * BIG, lanes), shift, preferred_element_type=F32
                    )
        for t in range(times):
            h = t // half
            by = {}
            for c in range(comps):
                x = w_ref[c, t, l].astype(F32)
                tiles = [x[g * SUB : (g + 1) * SUB] for g in range(groups)]
                up = [pltpu.roll(v, SUB - 1, 0) for v in tiles] + [0.0]
                down = [pltpu.roll(v, 1, 0) for v in tiles] + [0.0]
                for g in range(groups):
                    above = jnp.where(row == SUB - 1, up[g + 1], up[g])
                    below = jnp.where(row == 0, down[g - 1], down[g])
                    at = (t % half) * BIG + g % 2 * SUB
                    east = moved_s[h, c, g // 2, at : at + SUB, :lanes]
                    west = moved_s[h, c, g // 2, at : at + SUB, lanes:]
                    by[c, g] = ((above - below) * by_lon, east * by_up - west * by_down)
            cut = slice(t * SUB, (t + 1) * SUB)
            for g in range(groups):
                g_ref[l, 0, g, cut, :] = by[1, g][0] - by[0, g][1]
                g_ref[l, 1, g, cut, :] = by[0, g][0] + by[1, g][1]


def inner(winds, cos_rows, step_lon, step_lat):
    comps, times, levels, rows, lanes = winds.shape
    groups = rows // SUB
    thirds = rows // BIG
    deep = times * SUB
    whole = pl.BlockSpec(memory_space=pltpu.VMEM)
    elements = winds.size
    return pl.pallas_call(
        functools.partial(inner_kernel, step_lon, step_lat),
        in_specs=[whole] * 2,
        out_specs=[whole] * 2,
        out_shape=[
            jax.ShapeDtypeStruct((levels, 2, groups, deep, lanes), F32),
            jax.ShapeDtypeStruct((lanes, comps * thirds * 2 * lanes), BF16),
        ],
        scratch_shapes=[pltpu.VMEM((2, comps, thirds, times // 2 * BIG, 2 * lanes), F32)],
        compiler_params=pltpu.CompilerParams(vmem_limit_bytes=16 << 20),
        cost_estimate=pl.CostEstimate(
            flops=elements * 4 * lanes, transcendentals=0, bytes_accessed=elements * 6
        ),
        name="inner",
    )(winds, cos_rows)


def outer_kernel(
    step_lon, step_lat, g_ref, pick_ref, near_ref, far_ref, sidea_ref, sideb_ref, cos_ref,
    f_ref, c_ref, prev_s, next_s, halo_s,
):
    levels, _, groups, deep, lanes = g_ref.shape
    times = deep // SUB
    half = times // 2
    thirds = groups // 2
    comps = 2
    units = comps * thirds * 2
    by_lon, by_up, by_down = factors(cos_ref, step_lon, step_lat, (SUB, lanes))
    row = iota((SUB, lanes), 0)
    lane = iota((SUB, lanes), 1)
    by_lat = jnp.where(lane == lanes - 1, by_up, jnp.where(lane == 0, -by_down, 0.0))

    even = parity("lon_2") == 0
    near = near_ref[...].astype(F32)
    far = far_ref[...].astype(F32)
    lon_row = by_lon[0:1, :]
    prev_s[...] = jnp.where(even, far, near) * lon_row
    next_s[...] = jnp.where(even, near, far) * lon_row
    takes = (iota(sidea_ref.shape, 1) + parity("lat")) % 2 == 1
    side = jnp.where(takes, sidea_ref[...].astype(F32), sideb_ref[...].astype(F32))

    def lon_edge(c, t, l, g):
        k = (l * comps + c) * times + t
        if g == 0:
            return jnp.where(row == 0, -prev_s[k : k + 1, :], 0.0)
        if g == groups - 1:
            return jnp.where(row == SUB - 1, next_s[k : k + 1, :], 0.0)
        return None

    def one(t, l):
        h = t // half
        cut = slice(t * SUB, (t + 1) * SUB)
        vort, div = [], []
        for g in range(groups):
            at = (t % half) * BIG + g % 2 * SUB
            lat = []
            for c in range(comps):
                u = unit_of(c, g // 2, h, thirds) * lanes
                lat.append(halo_s[l % 2, at : at + SUB, u : u + lanes] * by_lat)
            first = g_ref[l, 0, g, cut, :] - lat[0]
            second = g_ref[l, 1, g, cut, :] + lat[1]
            if g in (0, groups - 1):
                first = first + lon_edge(1, t, l, g)
                second = second + lon_edge(0, t, l, g)
            vort.append(first)
            div.append(second)
        return vort, div

    total = None
    for l in range(levels):
        mine = side if l == 0 else pltpu.roll(side, lanes - 2 * units * l, 1)
        halo_s[l % 2] = jnp.dot(mine.astype(BF16), pick_ref[...], preferred_element_type=F32)
        for pair in range(times // 2):
            early, late = one(2 * pair, l), one(2 * pair + 1, l)
            at = pair * 2 * SUB
            for s in range(2):
                for g in range(groups):
                    both = jnp.concatenate([early[s][g], late[s][g]], axis=0)
                    f_ref[l, s, g, at : at + 2 * SUB, :] = both.astype(BF16)
        for s in range(2):
            x = jnp.concatenate([f_ref[l, s, g] for g in range(groups)], axis=1)
            term = lax.dot_general(x, x, (((1,), (1,)), ((), ())), preferred_element_type=F32)
            total = term if total is None else total + term

    same = iota((deep, deep), 0) % SUB == iota((deep, deep), 1) % SUB
    kept = jnp.where(same, total, 0.0)
    kept = kept.reshape(times, SUB, deep).sum(axis=1)
    fold = as_bf16(iota((deep, times), 0) // SUB == iota((deep, times), 1))
    cov = jnp.dot(
        jnp.concatenate(three_terms(kept), axis=1),
        jnp.concatenate([fold] * 3, axis=0),
        preferred_element_type=F32,
    )
    c_ref[...] = jnp.concatenate([cov[q * SUB : (q + 1) * SUB] for q in range(times // SUB)], axis=1)


def outer(g, pick, near, far, sidea, sideb, cos_rows, step_lon, step_lat):
    lanes = g.shape[-1]
    whole = pl.BlockSpec(memory_space=pltpu.VMEM)
    return pl.pallas_call(
        functools.partial(outer_kernel, step_lon, step_lat),
        in_specs=[whole] * 7,
        out_specs=[whole, whole],
        out_shape=[pltpu.VMEM(g.shape, BF16), jax.ShapeDtypeStruct((SUB, lanes), F32)],
        scratch_shapes=[
            pltpu.VMEM(near.shape, F32),
            pltpu.VMEM(near.shape, F32),
            pltpu.VMEM((2, sidea.shape[0], pick.shape[1]), F32),
        ],
        compiler_params=pltpu.CompilerParams(vmem_limit_bytes=16 << 20),
        name="outer",
    )(g, pick, near, far, sidea, sideb, cos_rows)


def transform(cov, table, total_rows, lanes):
    times = table.shape[1]
    half = lanes // 2
    table_b = table.astype(BF16)
    left = jnp.dot(
        jnp.concatenate([table_b] * 3, axis=1),
        jnp.concatenate(three_terms(cov), axis=0),
        preferred_element_type=F32,
    )
    gram = lax.dot_general(
        jnp.concatenate(three_terms(left), axis=1),
        jnp.concatenate([table_b] * 3, axis=1),
        (((1,), (1,)), ((), ())),
        preferred_element_type=F32,
    ) / total_rows
    row = iota((COLS, lanes), 0)
    lane = iota((COLS, lanes), 1)
    near = lane < half
    pad = jnp.zeros((COLS, half - COLS - times), F32)
    parts, sizes = [], []
    for f in range(FREQS):
        at = slice(f * COLS, (f + 1) * COLS)
        own = gram[at, at]
        diagonal = iota((COLS, COLS), 0) == iota((COLS, COLS), 1)
        size = jnp.max(jnp.where(diagonal, own, 0.0), axis=(0, 1), keepdims=True)
        sizes.append(size)
        parts += [own / size, table[at], pad]
    a = jnp.concatenate(parts, axis=1)

    for j in range(0, COLS, 2):
        c1 = jnp.where(near, a[:, j : j + 1], a[:, half + j : half + j + 1])
        c2 = jnp.where(near, a[:, j + 1 : j + 2], a[:, half + j + 1 : half + j + 2])
        r1 = a[j : j + 1, :]
        r2 = a[j + 1 : j + 2, :]
        p11 = c1[j : j + 1]
        p12 = c2[j : j + 1]
        p22 = c2[j + 1 : j + 2]
        inverse = 1.0 / (p11 * p22 - p12 * p12)
        s1 = (p22 * r1 - p12 * r2) * inverse
        s2 = (p11 * r2 - p12 * r1) * inverse
        a = jnp.where(row > j + 1, a - c1 * s1 - c2 * s2, a)

    odd = iota((COLS, 1), 0) % 2 == 1
    weights = []
    before = pltpu.roll(a, 1, 0)
    for f in range(FREQS):
        base = f * half
        on = jnp.sum(jnp.where(lane == base + row, a, 0.0), axis=1, keepdims=True)
        off = jnp.sum(jnp.where(lane == base + row - 1, a, 0.0), axis=1, keepdims=True)
        above = jnp.sum(jnp.where(lane == base + row - 1, before, 0.0), axis=1, keepdims=True)
        ratio = jnp.where(odd, off / above, 0.0)
        pivot = on - ratio * off
        cut = slice(base + COLS, base + COLS + times)
        weights.append((a[:, cut] - ratio * before[:, cut]) / jnp.sqrt(pivot) / jnp.sqrt(sizes[f]))
    return jnp.concatenate(weights, axis=0)


def basis_kernel(total_rows, sums_ref, table_ref, f_ref, out_hbm, out_ref, mix_ref, sems):
    levels, kinds, groups, deep, lanes = f_ref.shape
    times = deep // SUB
    outs = FREQS * COLS
    flat = jnp.sum(sums_ref[...], axis=0)
    cov = jnp.concatenate([flat[:, q * times : (q + 1) * times] for q in range(times // SUB)], axis=0)
    w = transform(cov, table_ref[...], total_rows, lanes)
    w_hi = w.astype(BF16)
    w_lo = (w - w_hi.astype(F32)).astype(BF16)
    spread = as_bf16(iota((outs * SUB, outs), 0) // SUB == iota((outs * SUB, outs), 1))
    widen = as_bf16(iota((times, deep), 0) == iota((times, deep), 1) // SUB)
    same = iota((outs * SUB, deep), 0) % SUB == iota((outs * SUB, deep), 1) % SUB
    for k, term in enumerate((w_hi, w_lo)):
        tall = jnp.dot(spread, term, preferred_element_type=F32).astype(BF16)
        full = jnp.dot(tall, widen, preferred_element_type=F32)
        mix_ref[:, k * deep : (k + 1) * deep] = jnp.where(same, full, 0.0).astype(BF16)

    @pl.loop(0, levels)
    def _(l):
        for s in range(kinds):
            for g in range(0, groups, 2):
                x = jnp.concatenate([f_ref[l, s, g], f_ref[l, s, g + 1]], axis=1)
                x = jnp.concatenate([x, x], axis=0)
                y = jnp.dot(mix_ref[...], x, preferred_element_type=F32)
                for e in range(2):
                    part = y[:, e * lanes : (e + 1) * lanes].reshape(outs, SUB, lanes)
                    out_ref[:, s, l, (g + e) * SUB : (g + e + 1) * SUB, :] = part
            pltpu.make_async_copy(out_ref.at[:, s, l], out_hbm.at[:, s, l], sems.at[s, l]).start()

    for l in range(levels):
        for s in range(kinds):
            pltpu.make_async_copy(out_ref.at[:, s, l], out_hbm.at[:, s, l], sems.at[s, l]).wait()


def basis_of(sums, table, f, total_rows):
    levels, kinds, groups, deep, lanes = f.shape
    outs = FREQS * COLS
    whole = pl.BlockSpec(memory_space=pltpu.VMEM)
    out_shape = (outs, kinds, levels, groups * SUB, lanes)
    return pl.pallas_call(
        functools.partial(basis_kernel, total_rows),
        in_specs=[whole, whole, whole],
        out_specs=pl.BlockSpec(memory_space=pltpu.HBM),
        out_shape=pltpu.HBM(out_shape, F32),
        scratch_shapes=[
            pltpu.VMEM(out_shape, F32),
            pltpu.VMEM((outs * SUB, 2 * deep), BF16),
            pltpu.SemaphoreType.DMA((kinds, levels)),
        ],
        compiler_params=pltpu.CompilerParams(vmem_limit_bytes=16 << 20),
        name="basis",
    )(sums, table, f)


def exchange(x, axes):
    copies = jnp.broadcast_to(x, (lax.axis_size(axes), *x.shape))
    return lax.all_to_all(copies, axes, split_axis=0, concat_axis=0, tiled=True)


def swap(x, axes, offset):
    size = lax.axis_size(axes)
    pairs = []
    for i in range(offset, size, 2):
        pairs += [(i, (i + 1) % size), ((i + 1) % size, i)]
    return lax.ppermute(x, axes, pairs)


def body(winds):
    _, times, levels, lon_cells, lat_cells = winds.shape
    grid_lon = lon_cells * lax.axis_size(LON)
    grid_lat = lat_cells * lax.axis_size("lat")
    step_lon = 2.0 * math.pi / grid_lon
    step_lat = 2.6 / grid_lat
    near, far, cols, winds = pack(winds)
    near = swap(near, "lon_2", 0)
    far = swap(far, LON, 1)
    cols, near = lax.optimization_barrier((cols, near))
    sidea = swap(cols, "lat", 0)
    sideb = swap(cols, "lat", 1)
    shape = (SUB, lat_cells)
    index = lax.axis_index("lat") * lat_cells + iota(shape, 1) + iota(shape, 0) - 1
    inside = (index >= 0) & (index < grid_lat)
    cos_rows = jnp.where(inside, jnp.cos(-1.3 + (index.astype(F32) + 0.5) * step_lat), 0.0)
    g, pick = inner(winds, cos_rows, step_lon, step_lat)
    f, cov = outer(g, pick, near, far, sidea, sideb, cos_rows, step_lon, step_lat)
    half_sums = exchange(cov, ("lon_2", "lat")).sum(axis=0)
    sums = exchange(half_sums, ("lon_0", "lon_1"))
    return basis_of(sums, jnp.asarray(taper_table()), f, 2 * levels * grid_lon * grid_lat)


def solution(mesh):
    split = Mesh(
        mesh.devices.reshape(4, 4, 2, mesh.shape["lat"]), ("lon_0", "lon_1", "lon_2", "lat")
    )
    placed = (P(None, None, None, LON, "lat"),)
    return jax.shard_map(
        body,
        mesh=split,
        in_specs=placed,
        out_specs=P(None, None, None, LON, "lat"),
        check_vma=False,
    )
```

```python
import functools
import math

import jax
import jax.numpy as jnp
import numpy as np
from jax import lax
from jax.experimental import pallas as pl
from jax.experimental.pallas import tpu as pltpu
from jax.sharding import Mesh
from jax.sharding import PartitionSpec as P

TIME = 32
TAPERS = 12
FREQS = 2
COLS = 2 * TAPERS
LON = ("lon_0", "lon_1", "lon_2")
SUB = 8
BIG = 16
F32 = jnp.float32
BF16 = jnp.bfloat16


def taper_table():
    t = np.arange(TIME, dtype=np.float32)
    k = np.arange(TAPERS, dtype=np.float32)
    weights = np.float32(math.sqrt(2.0 / (TIME + 1))) * np.sin(
        np.float32(math.pi)
        * (k[:, None] + np.float32(1.0))
        * (t[None, :] + np.float32(1.0))
        / np.float32(TIME + 1)
    )
    blocks = []
    for which in range(FREQS):
        phases = np.float32(2.0 * math.pi * (7 + 2 * which)) * t / np.float32(TIME)
        real_part = weights * np.cos(phases)[None, :]
        imag_part = -weights * np.sin(phases)[None, :]
        blocks.append(np.stack([real_part, imag_part], axis=1).reshape(COLS, TIME))
    return np.concatenate(blocks, axis=0).astype(jnp.bfloat16).astype(np.float32)


def iota(shape, dim):
    return lax.broadcasted_iota(jnp.int32, shape, dim)


def parity(axis):
    return lax.axis_index(axis) % 2


def as_bf16(mask):
    return mask.astype(F32).astype(BF16)


def three_terms(x):
    first = x.astype(BF16)
    rest = x - first.astype(F32)
    second = rest.astype(BF16)
    third = (rest - second.astype(F32)).astype(BF16)
    return first, second, third


def unit_of(c, g, h, thirds):
    return (c * thirds + g) * 2 + h


def pack_kernel(
    w_hbm, near_ref, far_ref, cols_ref, w_ref, first_s, last_s, acc_ref, sems,
):
    comps, times, levels, rows, lanes = w_ref.shape
    half = times // 2
    thirds = rows // BIG
    units = comps * thirds * 2
    copies = [
        pltpu.make_async_copy(w_hbm.at[:, :, l], w_ref.at[:, :, l], sems.at[l]) for l in range(levels)
    ]
    for copy in copies:
        copy.start()
    deep = half * BIG
    at = iota((units * lanes, lanes), 0)
    spot = iota((units * lanes, lanes), 1)
    here = at % lanes
    want = at // lanes * 2
    hit = as_bf16(((here == lanes - 1) & (spot == want)) | ((here == 0) & (spot == want + 1)))
    for l in range(levels):
        copies[l].wait()
        pieces = []
        for c in range(comps):
            for g in range(thirds):
                for h in range(2):
                    x = w_ref[c, h * half : (h + 1) * half, l, g * BIG : (g + 1) * BIG, :]
                    pieces.append(x.reshape(deep, lanes))
            for t in range(times):
                k = (l * comps + c) * times + t
                first_s[k : k + 1, :] = w_ref[c, t, l, 0:BIG, :].astype(F32)[0:1]
                last_s[k : k + 1, :] = w_ref[c, t, l, rows - BIG : rows, :].astype(F32)[BIG - 1 : BIG]
        total = jnp.dot(jnp.concatenate(pieces, axis=1), hit, preferred_element_type=F32)
        if l == 0:
            acc_ref[...] = total
        else:
            acc_ref[...] += pltpu.roll(total, 2 * units * l, 1)
    cols_ref[...] = acc_ref[...].astype(BF16)
    even = parity("lon_2") == 0
    near_ref[...] = jnp.where(even, last_s[...], first_s[...]).astype(BF16)
    far_ref[...] = jnp.where(even, first_s[...], last_s[...]).astype(BF16)


def pack(winds):
    comps, times, levels, rows, lanes = winds.shape
    deep = times // 2 * BIG
    many = levels * comps * times
    edge = jax.ShapeDtypeStruct((many, lanes), BF16)
    return pl.pallas_call(
        pack_kernel,
        in_specs=[pl.BlockSpec(memory_space=pltpu.HBM)],
        out_shape=[
            edge, edge, jax.ShapeDtypeStruct((deep, lanes), BF16), pltpu.VMEM(winds.shape, BF16),
        ],
        scratch_shapes=[
            pltpu.VMEM((many, lanes), F32),
            pltpu.VMEM((many, lanes), F32),
            pltpu.VMEM((deep, lanes), F32),
            pltpu.SemaphoreType.DMA((levels,)),
        ],
        compiler_params=pltpu.CompilerParams(vmem_limit_bytes=16 << 20),
        name="pack",
    )(pltpu.with_memory_space_constraint(winds, pltpu.HBM))


def factors(cos_ref, step_lon, step_lat, shape):
    cos_row = cos_ref[1:2, :]
    by_lon = jnp.broadcast_to(1.0 / (2.0 * step_lon) / cos_row, shape)
    by_up = jnp.broadcast_to(cos_ref[2:3, :] / (2.0 * step_lat) / cos_row, shape)
    by_down = jnp.broadcast_to(cos_ref[0:1, :] / (2.0 * step_lat) / cos_row, shape)
    return by_lon, by_up, by_down


def inner_kernel(step_lon, step_lat, w_ref, cos_ref, g_ref, pick_ref, moved_s):
    comps, times, levels, rows, lanes = w_ref.shape
    groups = rows // SUB
    thirds = rows // BIG
    half = times // 2
    by_lon, by_up, by_down = factors(cos_ref, step_lon, step_lat, (SUB, lanes))
    row = iota((SUB, lanes), 0)
    src = iota((lanes, lanes), 0)
    dst = iota((lanes, lanes), 1)
    shift = jnp.concatenate([as_bf16(src == dst + 1), as_bf16(src == dst - 1)], axis=1)

    wide = pick_ref.shape[1]
    src = iota((lanes, wide), 0)
    dst = iota((lanes, wide), 1)
    at = dst % lanes
    left = dst // lanes * 2
    pick_ref[...] = as_bf16(((at == 0) & (src == left)) | ((at == lanes - 1) & (src == left + 1)))

    for l in range(levels):
        for h in range(2):
            for c in range(comps):
                for g in range(thirds):
                    x = w_ref[c, h * half : (h + 1) * half, l, g * BIG : (g + 1) * BIG, :]
                    moved_s[h, c, g] = jnp.dot(
                        x.reshape(half * BIG, lanes), shift, preferred_element_type=F32
                    )
        for t in range(times):
            h = t // half
            by = {}
            for c in range(comps):
                x = w_ref[c, t, l].astype(F32)
                tiles = [x[g * SUB : (g + 1) * SUB] for g in range(groups)]
                up = [pltpu.roll(v, SUB - 1, 0) for v in tiles] + [0.0]
                down = [pltpu.roll(v, 1, 0) for v in tiles] + [0.0]
                for g in range(groups):
                    above = jnp.where(row == SUB - 1, up[g + 1], up[g])
                    below = jnp.where(row == 0, down[g - 1], down[g])
                    at = (t % half) * BIG + g % 2 * SUB
                    east = moved_s[h, c, g // 2, at : at + SUB, :lanes]
                    west = moved_s[h, c, g // 2, at : at + SUB, lanes:]
                    by[c, g] = ((above - below) * by_lon, east * by_up - west * by_down)
            cut = slice(t * SUB, (t + 1) * SUB)
            for g in range(groups):
                g_ref[l, 0, g, cut, :] = by[1, g][0] - by[0, g][1]
                g_ref[l, 1, g, cut, :] = by[0, g][0] + by[1, g][1]


def inner(winds, cos_rows, step_lon, step_lat):
    comps, times, levels, rows, lanes = winds.shape
    groups = rows // SUB
    thirds = rows // BIG
    deep = times * SUB
    whole = pl.BlockSpec(memory_space=pltpu.VMEM)
    elements = winds.size
    return pl.pallas_call(
        functools.partial(inner_kernel, step_lon, step_lat),
        in_specs=[whole] * 2,
        out_specs=[whole] * 2,
        out_shape=[
            jax.ShapeDtypeStruct((levels, 2, groups, deep, lanes), F32),
            jax.ShapeDtypeStruct((lanes, comps * thirds * 2 * lanes), BF16),
        ],
        scratch_shapes=[pltpu.VMEM((2, comps, thirds, times // 2 * BIG, 2 * lanes), F32)],
        compiler_params=pltpu.CompilerParams(vmem_limit_bytes=16 << 20),
        cost_estimate=pl.CostEstimate(
            flops=elements * 4 * lanes, transcendentals=0, bytes_accessed=elements * 6
        ),
        name="inner",
    )(winds, cos_rows)


def outer_kernel(
    step_lon, step_lat, g_ref, pick_ref, near_ref, far_ref, sidea_ref, sideb_ref, cos_ref,
    f_ref, c_ref, prev_s, next_s, halo_s,
):
    levels, _, groups, deep, lanes = g_ref.shape
    times = deep // SUB
    half = times // 2
    thirds = groups // 2
    comps = 2
    units = comps * thirds * 2
    by_lon, by_up, by_down = factors(cos_ref, step_lon, step_lat, (SUB, lanes))
    row = iota((SUB, lanes), 0)
    lane = iota((SUB, lanes), 1)
    by_lat = jnp.where(lane == lanes - 1, by_up, jnp.where(lane == 0, -by_down, 0.0))

    even = parity("lon_2") == 0
    near = near_ref[...].astype(F32)
    far = far_ref[...].astype(F32)
    lon_row = by_lon[0:1, :]
    prev_s[...] = jnp.where(even, far, near) * lon_row
    next_s[...] = jnp.where(even, near, far) * lon_row
    takes = (iota(sidea_ref.shape, 1) + parity("lat")) % 2 == 1
    side = jnp.where(takes, sidea_ref[...].astype(F32), sideb_ref[...].astype(F32))

    def lon_edge(c, t, l, g):
        k = (l * comps + c) * times + t
        if g == 0:
            return jnp.where(row == 0, -prev_s[k : k + 1, :], 0.0)
        if g == groups - 1:
            return jnp.where(row == SUB - 1, next_s[k : k + 1, :], 0.0)
        return None

    def one(t, l):
        h = t // half
        cut = slice(t * SUB, (t + 1) * SUB)
        vort, div = [], []
        for g in range(groups):
            at = (t % half) * BIG + g % 2 * SUB
            lat = []
            for c in range(comps):
                u = unit_of(c, g // 2, h, thirds) * lanes
                lat.append(halo_s[l % 2, at : at + SUB, u : u + lanes] * by_lat)
            first = g_ref[l, 0, g, cut, :] - lat[0]
            second = g_ref[l, 1, g, cut, :] + lat[1]
            if g in (0, groups - 1):
                first = first + lon_edge(1, t, l, g)
                second = second + lon_edge(0, t, l, g)
            vort.append(first)
            div.append(second)
        return vort, div

    total = None
    for l in range(levels):
        mine = side if l == 0 else pltpu.roll(side, lanes - 2 * units * l, 1)
        halo_s[l % 2] = jnp.dot(mine.astype(BF16), pick_ref[...], preferred_element_type=F32)
        for pair in range(times // 2):
            early, late = one(2 * pair, l), one(2 * pair + 1, l)
            at = pair * 2 * SUB
            for s in range(2):
                for g in range(groups):
                    both = jnp.concatenate([early[s][g], late[s][g]], axis=0)
                    f_ref[l, s, g, at : at + 2 * SUB, :] = both.astype(BF16)
        for s in range(2):
            x = jnp.concatenate([f_ref[l, s, g] for g in range(groups)], axis=1)
            term = lax.dot_general(x, x, (((1,), (1,)), ((), ())), preferred_element_type=F32)
            total = term if total is None else total + term

    same = iota((deep, deep), 0) % SUB == iota((deep, deep), 1) % SUB
    kept = jnp.where(same, total, 0.0)
    kept = kept.reshape(times, SUB, deep).sum(axis=1)
    fold = as_bf16(iota((deep, times), 0) // SUB == iota((deep, times), 1))
    cov = jnp.dot(
        jnp.concatenate(three_terms(kept), axis=1),
        jnp.concatenate([fold] * 3, axis=0),
        preferred_element_type=F32,
    )
    c_ref[...] = jnp.concatenate([cov[q * SUB : (q + 1) * SUB] for q in range(times // SUB)], axis=1)


def outer(g, pick, near, far, sidea, sideb, cos_rows, step_lon, step_lat):
    lanes = g.shape[-1]
    whole = pl.BlockSpec(memory_space=pltpu.VMEM)
    return pl.pallas_call(
        functools.partial(outer_kernel, step_lon, step_lat),
        in_specs=[whole] * 7,
        out_specs=[whole, whole],
        out_shape=[pltpu.VMEM(g.shape, BF16), jax.ShapeDtypeStruct((SUB, lanes), F32)],
        scratch_shapes=[
            pltpu.VMEM(near.shape, F32),
            pltpu.VMEM(near.shape, F32),
            pltpu.VMEM((2, sidea.shape[0], pick.shape[1]), F32),
        ],
        compiler_params=pltpu.CompilerParams(vmem_limit_bytes=16 << 20),
        name="outer",
    )(g, pick, near, far, sidea, sideb, cos_rows)


def transform(cov, table, total_rows, lanes):
    times = table.shape[1]
    half = lanes // 2
    table_b = table.astype(BF16)
    left = jnp.dot(
        jnp.concatenate([table_b] * 3, axis=1),
        jnp.concatenate(three_terms(cov), axis=0),
        preferred_element_type=F32,
    )
    gram = lax.dot_general(
        jnp.concatenate(three_terms(left), axis=1),
        jnp.concatenate([table_b] * 3, axis=1),
        (((1,), (1,)), ((), ())),
        preferred_element_type=F32,
    ) / total_rows
    row = iota((COLS, lanes), 0)
    lane = iota((COLS, lanes), 1)
    near = lane < half
    pad = jnp.zeros((COLS, half - COLS - times), F32)
    parts, sizes = [], []
    for f in range(FREQS):
        at = slice(f * COLS, (f + 1) * COLS)
        own = gram[at, at]
        diagonal = iota((COLS, COLS), 0) == iota((COLS, COLS), 1)
        size = jnp.max(jnp.where(diagonal, own, 0.0), axis=(0, 1), keepdims=True)
        sizes.append(size)
        parts += [own / size, table[at], pad]
    a = jnp.concatenate(parts, axis=1)

    for j in range(0, COLS, 2):
        c1 = jnp.where(near, a[:, j : j + 1], a[:, half + j : half + j + 1])
        c2 = jnp.where(near, a[:, j + 1 : j + 2], a[:, half + j + 1 : half + j + 2])
        r1 = a[j : j + 1, :]
        r2 = a[j + 1 : j + 2, :]
        p11 = c1[j : j + 1]
        p12 = c2[j : j + 1]
        p22 = c2[j + 1 : j + 2]
        inverse = 1.0 / (p11 * p22 - p12 * p12)
        s1 = (p22 * r1 - p12 * r2) * inverse
        s2 = (p11 * r2 - p12 * r1) * inverse
        a = jnp.where(row > j + 1, a - c1 * s1 - c2 * s2, a)

    odd = iota((COLS, 1), 0) % 2 == 1
    weights = []
    before = pltpu.roll(a, 1, 0)
    for f in range(FREQS):
        base = f * half
        on = jnp.sum(jnp.where(lane == base + row, a, 0.0), axis=1, keepdims=True)
        off = jnp.sum(jnp.where(lane == base + row - 1, a, 0.0), axis=1, keepdims=True)
        above = jnp.sum(jnp.where(lane == base + row - 1, before, 0.0), axis=1, keepdims=True)
        ratio = jnp.where(odd, off / above, 0.0)
        pivot = on - ratio * off
        cut = slice(base + COLS, base + COLS + times)
        weights.append((a[:, cut] - ratio * before[:, cut]) / jnp.sqrt(pivot) / jnp.sqrt(sizes[f]))
    return jnp.concatenate(weights, axis=0)


def basis_kernel(total_rows, sums_ref, table_ref, f_ref, out_hbm, out_ref, mix_ref, sems):
    levels, kinds, groups, deep, lanes = f_ref.shape
    times = deep // SUB
    outs = FREQS * COLS
    flat = jnp.sum(sums_ref[...], axis=0)
    cov = jnp.concatenate([flat[:, q * times : (q + 1) * times] for q in range(times // SUB)], axis=0)
    w = transform(cov, table_ref[...], total_rows, lanes)
    w_hi = w.astype(BF16)
    w_lo = (w - w_hi.astype(F32)).astype(BF16)
    spread = as_bf16(iota((outs * SUB, outs), 0) // SUB == iota((outs * SUB, outs), 1))
    widen = as_bf16(iota((times, deep), 0) == iota((times, deep), 1) // SUB)
    same = iota((outs * SUB, deep), 0) % SUB == iota((outs * SUB, deep), 1) % SUB
    for k, term in enumerate((w_hi, w_lo)):
        tall = jnp.dot(spread, term, preferred_element_type=F32).astype(BF16)
        full = jnp.dot(tall, widen, preferred_element_type=F32)
        mix_ref[:, k * deep : (k + 1) * deep] = jnp.where(same, full, 0.0).astype(BF16)

    for l in range(levels):
        for s in range(kinds):
            for g in range(0, groups, 2):
                x = jnp.concatenate([f_ref[l, s, g], f_ref[l, s, g + 1]], axis=1)
                x = jnp.concatenate([x, x], axis=0)
                y = jnp.dot(mix_ref[...], x, preferred_element_type=F32)
                for e in range(2):
                    part = y[:, e * lanes : (e + 1) * lanes].reshape(outs, SUB, lanes)
                    out_ref[:, s, l, (g + e) * SUB : (g + e + 1) * SUB, :] = part
            pltpu.make_async_copy(out_ref.at[:, s, l], out_hbm.at[:, s, l], sems.at[s, l]).start()

    for l in range(levels):
        for s in range(kinds):
            pltpu.make_async_copy(out_ref.at[:, s, l], out_hbm.at[:, s, l], sems.at[s, l]).wait()


def basis_of(sums, table, f, total_rows):
    levels, kinds, groups, deep, lanes = f.shape
    outs = FREQS * COLS
    whole = pl.BlockSpec(memory_space=pltpu.VMEM)
    out_shape = (outs, kinds, levels, groups * SUB, lanes)
    return pl.pallas_call(
        functools.partial(basis_kernel, total_rows),
        in_specs=[whole, whole, whole],
        out_specs=pl.BlockSpec(memory_space=pltpu.HBM),
        out_shape=pltpu.HBM(out_shape, F32),
        scratch_shapes=[
            pltpu.VMEM(out_shape, F32),
            pltpu.VMEM((outs * SUB, 2 * deep), BF16),
            pltpu.SemaphoreType.DMA((kinds, levels)),
        ],
        compiler_params=pltpu.CompilerParams(vmem_limit_bytes=16 << 20),
        name="basis",
    )(sums, table, f)


def exchange(x, axes):
    copies = jnp.broadcast_to(x, (lax.axis_size(axes), *x.shape))
    return lax.all_to_all(copies, axes, split_axis=0, concat_axis=0, tiled=True)


def swap(x, axes, offset):
    size = lax.axis_size(axes)
    pairs = []
    for i in range(offset, size, 2):
        pairs += [(i, (i + 1) % size), ((i + 1) % size, i)]
    return lax.ppermute(x, axes, pairs)


def body(winds):
    _, times, levels, lon_cells, lat_cells = winds.shape
    grid_lon = lon_cells * lax.axis_size(LON)
    grid_lat = lat_cells * lax.axis_size("lat")
    step_lon = 2.0 * math.pi / grid_lon
    step_lat = 2.6 / grid_lat
    near, far, cols, winds = pack(winds)
    near = swap(near, "lon_2", 0)
    far = swap(far, LON, 1)
    cols, near = lax.optimization_barrier((cols, near))
    sidea = swap(cols, "lat", 0)
    sideb = swap(cols, "lat", 1)
    shape = (SUB, lat_cells)
    index = lax.axis_index("lat") * lat_cells + iota(shape, 1) + iota(shape, 0) - 1
    inside = (index >= 0) & (index < grid_lat)
    cos_rows = jnp.where(inside, jnp.cos(-1.3 + (index.astype(F32) + 0.5) * step_lat), 0.0)
    g, pick = inner(winds, cos_rows, step_lon, step_lat)
    f, cov = outer(g, pick, near, far, sidea, sideb, cos_rows, step_lon, step_lat)
    half_sums = exchange(cov, ("lon_2", "lat")).sum(axis=0)
    sums = exchange(half_sums, ("lon_0", "lon_1"))
    return basis_of(sums, jnp.asarray(taper_table()), f, 2 * levels * grid_lon * grid_lat)


def solution(mesh):
    split = Mesh(
        mesh.devices.reshape(4, 4, 2, mesh.shape["lat"]), ("lon_0", "lon_1", "lon_2", "lat")
    )
    placed = (P(None, None, None, LON, "lat"),)
    return jax.shard_map(
        body,
        mesh=split,
        in_specs=placed,
        out_specs=P(None, None, None, LON, "lat"),
        check_vma=False,
    )
```
